32 devices in a mesh: outer: 8 (over z, core), inner: 4 (over y, x).
Axes of the slice: x: 2, y: 2, z: 4, core: 2. Of those that a mesh axis runs over, the one named last changes fastest.
Arguments:
- queries: bfloat16 [65536, 512], P(('outer', 'inner')), may hold values from -6 to 6
- inv_sqrt_degree: float32 [65536], P(('outer', 'inner')), may hold values from 0.35 to 1
- leaf_blocks: bfloat16 [512, 12, 128, 128], P(('outer', 'inner')), may hold values from -0.15625 to 0.15625
- block_cols: int32 [512, 12], P(('outer', 'inner')), may hold values from 0 to 15, as said below
- left_upper: bfloat16 [65536, 128], P(('outer', 'inner')), may hold values from -0.5 to 0.5
- right_upper: bfloat16 [65536, 128], P(('outer', 'inner')), may hold values from -0.03125 to 0.03125
- left_lower: bfloat16 [65536, 128], P(('outer', 'inner')), may hold values from -0.5 to 0.5
- right_lower: bfloat16 [65536, 128], P(('outer', 'inner')), may hold values from -0.09375 to 0.09375
Outputs:
- ranking: float32 [65536, 512], P(('outer', 'inner'))
The draws below stay inside these ranges and needn't reach their ends.
Inputs may be any that keep to these rules, and one draw needn't show every extreme that they name: `block_cols`: in each block row the 12 block columns are distinct and count blocks from the first row of the same device's 2048 rows; the first of them is the row's own block.
All inputs are finite; a program needn't handle non-finite values.
Results may differ from the reference program's by a relative error of at most 0.0033.
Values sent between devices are 32-bit elements; how exact they have to be, the bound alone decides.
No kernel may reach another device: no remote copies, remote signals or barrier semaphores. Data moves between devices by JAX's collectives and lax.ppermute only.
A program may use at most 64 MiB of HBM per device.

```python
import math
import jax
import jax.numpy as jnp
from jax import lax

ROWS_DEV = 2048
QUERIES = 512
RANK = 128
BLOCK = 128
NB = 12
ITERS = 2
ROWS = 65536
BLOCK_ROWS = 512
N_OUTER = 8
N_INNER = 4


def draw_block_cols(key, part):
    leaf_count = ROWS_DEV // BLOCK
    scores = jax.random.randint(key, (BLOCK_ROWS, leaf_count - 1), 0, 1048576) * leaf_count
    scores = scores + jnp.arange(leaf_count - 1, dtype=jnp.int32)[None, :]
    chosen = lax.top_k(scores, NB - 1)[1].astype(jnp.int32) + 1
    offsets = jnp.concatenate([jnp.zeros((BLOCK_ROWS, 1), jnp.int32), chosen], axis=1)
    own = (jnp.arange(BLOCK_ROWS, dtype=jnp.int32) % leaf_count)[:, None]
    return ((own + offsets) % leaf_count).astype(jnp.int32)


def shard_levels(rng, shape, cuts, low, high):
    gain, own = 1.0, jax.random.fold_in(rng, 6)
    for dim, parts in cuts:
        heights = jnp.exp(jax.random.uniform(jax.random.fold_in(own, dim), (parts,), jnp.float32, low / len(cuts), high / len(cuts)))
        gain = gain * jnp.repeat(heights, shape[dim] // parts).reshape([-1 if axis == dim else 1 for axis in range(len(shape))])
    return gain


def noise(own_key, extent, width, limit, shards=(), kind=jnp.bfloat16):
    factor_of = shard_levels(own_key, extent, shards, -0.22, 0.18) if shards else 1.0
    drawn = jax.random.normal(own_key, extent, jnp.float32) * width * factor_of
    return jnp.minimum(jnp.maximum(drawn, -limit), limit).astype(kind)


def setup_inputs(seed: int = 0) -> dict:
    key_of = jax.random.split(jax.random.key(seed), 9)
    return {
        "queries": noise(key_of[0], (ROWS, QUERIES), 1.0, 6.0, ((0, 32),)),
        "inv_sqrt_degree": jnp.clip(jnp.exp(math.log(1.0) - 1.0498221 * jax.random.uniform(key_of[1], (ROWS,), jnp.float32) ** shard_levels(key_of[1], (ROWS,), ((0, 32),), -0.2, 0.2)), 0.35, 1.0),
        "leaf_blocks": noise(key_of[2], (BLOCK_ROWS, NB, BLOCK, BLOCK), (NB * BLOCK) ** -0.5, 0.15625, ((0, 32),)),
        "block_cols": draw_block_cols(jax.random.fold_in(key_of[8], 71), 0),
        "left_upper": noise(key_of[4], (ROWS, RANK), RANK ** -0.5, 0.5, ((0, 32),)),
        "right_upper": noise(key_of[5], (ROWS, RANK), (ROWS // 2) ** -0.5, 0.03125, ((0, 32),)),
        "left_lower": noise(key_of[6], (ROWS, RANK), RANK ** -0.5, 0.5, ((0, 32),)),
        "right_lower": noise(key_of[7], (ROWS, RANK), (ROWS_DEV * N_INNER // 2) ** -0.5, 0.09375, ((0, 32),)),
    }


damping = 0.9

def reference(queries, inv_sqrt_degree, leaf_blocks, block_cols, left_upper, right_upper, left_lower, right_lower):
    devices = N_OUTER * N_INNER
    leaf_count = ROWS_DEV // BLOCK
    iterate = queries.astype(jnp.float32)
    queries_dev = queries.reshape(devices, ROWS_DEV, QUERIES)
    degree_dev = inv_sqrt_degree.reshape(devices, ROWS_DEV)
    blocks_dev = leaf_blocks.reshape(devices, leaf_count, NB, BLOCK, BLOCK)
    cols_dev = block_cols.reshape(devices, leaf_count, NB)
    lu_dev = left_upper.reshape(devices, ROWS_DEV, RANK)
    ru_dev = right_upper.reshape(devices, ROWS_DEV, RANK)
    ll_dev = left_lower.reshape(devices, ROWS_DEV, RANK)
    rl_dev = right_lower.reshape(devices, ROWS_DEV, RANK)
    for sweep in range(ITERS):
        scaled = (inv_sqrt_degree[:, None] * iterate).astype(jnp.bfloat16)
        scaled_dev = scaled.reshape(devices, ROWS_DEV, QUERIES)

        def partial_terms(pieces):
            scaled_one, right_up, right_low = pieces
            return (jnp.dot(right_up.T, scaled_one, preferred_element_type=jnp.float32), jnp.dot(right_low.T, scaled_one, preferred_element_type=jnp.float32))
        upper_part, lower_part = lax.map(partial_terms, (scaled_dev, ru_dev, rl_dev))
        upper_sum = upper_part.reshape(2, devices // 2, RANK, QUERIES).sum(axis=1)
        lower_sum = lower_part.reshape(N_OUTER, 2, N_INNER // 2, RANK, QUERIES).sum(axis=2)
        upper_sib = (damping * upper_sum[::-1]).astype(jnp.bfloat16)
        lower_sib = (damping * lower_sum[:, ::-1]).astype(jnp.bfloat16)
        upper_each = jnp.repeat(upper_sib, devices // 2, axis=0)
        lower_each = jnp.broadcast_to(lower_sib[:, :, None], (N_OUTER, 2, N_INNER // 2, RANK, QUERIES)).reshape(devices, RANK, QUERIES)

        def update(pieces):
            blocks, cols, scaled_one, left_up, left_low, coef_up, coef_low, query_one, degree_one = pieces
            scaled_blocks = scaled_one.reshape(leaf_count, BLOCK, QUERIES)
            picked = scaled_blocks[cols].astype(jnp.float32)
            leaf_term = jnp.einsum('bjxy,bjyq->bxq', blocks.astype(jnp.float32), picked).reshape(ROWS_DEV, QUERIES)
            coupled = jnp.dot(left_up, coef_up, preferred_element_type=jnp.float32) + jnp.dot(left_low, coef_low, preferred_element_type=jnp.float32)
            return query_one.astype(jnp.float32) + degree_one[:, None] * (damping * leaf_term + coupled)
        iterate = lax.map(update, (blocks_dev, cols_dev, scaled_dev, lu_dev, ll_dev, upper_each, lower_each, queries_dev, degree_dev)).reshape(ROWS, QUERIES)
    return iterate
```

```python
import jax
import jax.numpy as jnp
from jax import lax
from jax.experimental import pallas as pl
from jax.experimental.pallas import tpu as pltpu
from jax.sharding import Mesh
from jax.sharding import PartitionSpec as P

DAMPING = 0.9
F32 = jnp.float32
BF16 = jnp.bfloat16
VMEM = pl.BlockSpec(memory_space=pltpu.VMEM)
SMEM = pl.BlockSpec(memory_space=pltpu.SMEM)
FAR = pl.BlockSpec(memory_space=pltpu.HBM)


def shape(dims, dtype, near=False):
    return (pltpu.VMEM if near else pltpu.HBM)(dims, dtype)


def call(kernel, args, outs, scratch, megabytes, flops):
    values = [
        value if spec is SMEM else pltpu.with_memory_space_constraint(value, spec.memory_space)
        for value, spec in args
    ]
    return pl.pallas_call(
        kernel,
        out_shape=[out for out in outs],
        in_specs=[spec for _, spec in args],
        out_specs=[
            FAR if out.memory_space == pltpu.HBM else VMEM for out in outs
        ],
        scratch_shapes=scratch,
        cost_estimate=pl.CostEstimate(
            flops=flops, bytes_accessed=2**20, transcendentals=0
        ),
        compiler_params=pltpu.CompilerParams(vmem_limit_bytes=megabytes * 2**20),
    )(*values)


def dot(a, b):
    return jnp.dot(a, b, preferred_element_type=F32)


def tdot(a, b):
    return lax.dot_general(a, b, (((0,), (0,)), ((), ())), preferred_element_type=F32)


def start(source, target, sem):
    copy = pltpu.make_async_copy(source, target, sem)
    copy.start()
    return copy


def degree_columns(degree_ref):
    leaves, block = degree_ref.shape
    tall = jnp.concatenate([degree_ref[...]] * (block // leaves), axis=0)
    return tall.T[:, :leaves]


def scale_tile(columns, first, value):
    block = columns.shape[0]
    return jnp.concatenate(
        [
            columns[:, first + b : first + b + 1] * value[b * block : (b + 1) * block]
            for b in range(value.shape[0] // block)
        ],
        axis=0,
    )


def coupling_kernel(
    degree_hbm, lu_hbm, ll_hbm, ru_hbm, rl_hbm,
    spread_hbm, right_hbm, late_hbm, early_ref,
    degree_ref, lu_ref, ll_ref, ru_ref, rl_ref, spread_ref, right_ref, late_ref, sems,
):
    pairs = (
        (degree_hbm, degree_ref), (ll_hbm, ll_ref), (ru_hbm, ru_ref), (lu_hbm, lu_ref), (rl_hbm, rl_ref),
    )
    copies = [start(a, b, sems.at[i]) for i, (a, b) in enumerate(pairs)]
    leaves, block = degree_ref.shape
    rank = lu_ref.shape[1]
    copies[0].wait()
    columns = degree_columns(degree_ref)
    square = columns * columns

    def scaled(source, target, lanes):
        for leaf in range(leaves):
            rows = slice(leaf * block, (leaf + 1) * block)
            target[rows, lanes] = (
                square[:, leaf : leaf + 1] * source[rows, :].astype(F32)
            ).astype(BF16)

    copies[1].wait()
    scaled(ll_ref, spread_ref, slice(rank, 2 * rank))
    copies[2].wait()
    early_ref[...] = tdot(spread_ref[:, rank:], ru_ref[...])
    scaled(ru_ref, right_ref, slice(0, rank))
    copies[3].wait()
    scaled(lu_ref, spread_ref, slice(0, rank))
    out0 = start(spread_ref, spread_hbm, sems.at[5])
    late_ref[:rank, :] = tdot(spread_ref[:, :rank], ru_ref[...])
    copies[4].wait()
    scaled(rl_ref, right_ref, slice(rank, 2 * rank))
    out1 = start(right_ref, right_hbm, sems.at[6])
    late_ref[rank:, :] = tdot(spread_ref[...], rl_ref[...])
    out2 = start(late_ref, late_hbm, sems.at[7])
    for out in (out0, out1, out2):
        out.wait()


def first_kernel(
    degree_hbm, y_hbm, ru_hbm, rl_hbm,
    scaled_hbm, coef_hbm, lower_ref,
    degree_ref, y_ref, right_ref, scaled_ref, coef_ref, sems,
):
    leaves, block = degree_ref.shape
    rank = ru_hbm.shape[1]
    tiles = 4
    size = y_ref.shape[0] // tiles
    copies = [start(degree_hbm, degree_ref, sems.at[0])]
    for tile in range(tiles):
        rows = pl.ds(tile * size, size)
        copies.append(start(y_hbm.at[rows], y_ref.at[rows], sems.at[1 + tile]))
    sides = [
        start(ru_hbm, right_ref.at[:, pl.ds(0, rank)], sems.at[9]),
        start(rl_hbm, right_ref.at[:, pl.ds(rank, rank)], sems.at[10]),
    ]
    copies[0].wait()
    columns = degree_columns(degree_ref)
    outs = []
    for tile in range(tiles):
        copies[1 + tile].wait()
        rows = slice(tile * size, (tile + 1) * size)
        value = y_ref[rows, :].astype(F32)
        scaled_ref[rows, :] = scale_tile(columns, tile * size // block, value).astype(BF16)
        near = pl.ds(tile * size, size)
        outs.append(start(scaled_ref.at[near], scaled_hbm.at[near], sems.at[5 + tile]))
    for copy in sides:
        copy.wait()
    coef_ref[...] = tdot(scaled_ref[...], right_ref[...])
    outs.append(start(coef_ref, coef_hbm, sems.at[0]))
    lower_ref[...] = coef_ref[:, rank:]
    for out in outs:
        out.wait()


def dense_kernel(
    cols_ref, blocks_hbm, scaled_hbm, right_hbm, coef_hbm, late_hbm, cross_ref,
    dense_hbm, low_hbm, both_ref,
    blocks_ref, dense_ref, scaled_ref, right_ref, coef_ref, late_ref, low_ref, sems,
):
    leaves, stored, block, _ = blocks_ref.shape
    copies = [
        start(blocks_hbm.at[row], blocks_ref.at[row], sems.at[row])
        for row in range(leaves)
    ]
    sides = [
        start(a, b, sems.at[leaves + i])
        for i, (a, b) in enumerate(
            ((right_hbm, right_ref), (scaled_hbm, scaled_ref), (coef_hbm, coef_ref), (late_hbm, late_ref))
        )
    ]
    outs = []
    for row in range(leaves):
        rows = slice(row * block, (row + 1) * block)
        dense_ref[rows, :] = jnp.zeros((block, leaves * block), BF16)
        copies[row].wait()
        for j in range(stored):
            col = pl.multiple_of(cols_ref[row, j] * block, block)
            dense_ref[rows, pl.ds(col, block)] = blocks_ref[row, j]
        near = pl.ds(row * block, block)
        outs.append(start(dense_ref.at[near], dense_hbm.at[near], sems.at[row]))
    for side in sides:
        side.wait()
    rank = cross_ref.shape[0]
    parts, height, _ = both_ref.shape
    through = tdot(right_ref[...], dense_ref[...]).astype(BF16)
    found = coef_ref[...] + DAMPING * dot(through, scaled_ref[...]).T
    second = found[:, :rank] + dot(
        coef_ref[:, rank:].astype(BF16), (DAMPING * cross_ref[...]).astype(BF16)
    )
    low_ref[: found.shape[0], :] = found[:, rank:]
    low_ref[found.shape[0] :, :] = late_ref[rank:, :]
    outs.append(start(low_ref, low_hbm, sems.at[leaves]))
    width = found.shape[0] // parts
    lines = rank // parts
    both_ref[:, :width, :] = coef_ref[:, :rank].reshape(parts, width, rank)
    both_ref[:, width : 2 * width, :] = second.reshape(parts, width, rank)
    for part in range(parts):
        both_ref[part, 2 * width : 2 * width + lines, :] = late_ref[
            part * lines : (part + 1) * lines, :
        ]
    for out in outs:
        out.wait()


def load_tiles(hbm, ref, tiles, sems, first):
    size = ref.shape[0] // tiles
    return [
        start(hbm.at[pl.ds(t * size, size)], ref.at[pl.ds(t * size, size)], sems.at[first + t])
        for t in range(tiles)
    ]


def known_kernel(
    degree_hbm, dense_hbm, scaled_hbm, spread_hbm, y_hbm,
    known_hbm, far_hbm,
    degree_ref, dense_ref, scaled_ref, spread_ref, y_ref, known_ref, far_ref, sems,
):
    tiles = 8
    block = degree_ref.shape[1]
    size = dense_ref.shape[0] // tiles
    sides = [
        start(a, b, sems.at[tiles + i])
        for i, (a, b) in enumerate(
            ((degree_hbm, degree_ref), (scaled_hbm, scaled_ref), (spread_hbm, spread_ref), (y_hbm, y_ref))
        )
    ]
    copies = load_tiles(dense_hbm, dense_ref, tiles, sems, 0)
    for side in sides:
        side.wait()
    columns = degree_columns(degree_ref)
    outs = []
    for tile in range(tiles):
        rows = slice(tile * size, (tile + 1) * size)
        near = pl.ds(tile * size, size)
        copies[tile].wait()
        product = dot(dense_ref[rows, :], scaled_ref[...])
        first = tile * size // block
        value = y_ref[rows, :].astype(F32) + DAMPING * scale_tile(columns, first, product)
        known_ref[rows, :] = scale_tile(columns, first, value).astype(BF16)
        far_ref[rows, :] = (DAMPING * dot(dense_ref[rows, :], spread_ref[...])).astype(BF16)
        outs.append(start(known_ref.at[near], known_hbm.at[near], sems.at[tile]))
        outs.append(start(far_ref.at[near], far_hbm.at[near], sems.at[tiles + tile]))
    for out in outs:
        out.wait()


def base_kernel(
    degree_hbm, dense_hbm, known_hbm, y_hbm,
    base_hbm,
    degree_ref, dense_ref, known_ref, y_ref, base_ref, sems,
):
    tiles = 8
    block = degree_ref.shape[1]
    size = dense_ref.shape[0] // tiles
    sides = [
        start(a, b, sems.at[tiles + i])
        for i, (a, b) in enumerate(
            ((degree_hbm, degree_ref), (known_hbm, known_ref), (y_hbm, y_ref))
        )
    ]
    copies = load_tiles(dense_hbm, dense_ref, tiles, sems, 0)
    for side in sides:
        side.wait()
    columns = degree_columns(degree_ref)
    outs = []
    for tile in range(tiles):
        rows = slice(tile * size, (tile + 1) * size)
        near = pl.ds(tile * size, size)
        copies[tile].wait()
        product = dot(dense_ref[rows, :], known_ref[...])
        base_ref[rows, :] = y_ref[rows, :].astype(F32) + DAMPING * scale_tile(
            columns, tile * size // block, product
        )
        outs.append(start(base_ref.at[near], base_hbm.at[near], sems.at[tile]))
    for out in outs:
        out.wait()


def final_kernel(
    degree_hbm, base_hbm, far_hbm, lu_hbm, ll_hbm, upper_ref, own_ref, sib_ref, low_ref,
    out_hbm,
    degree_ref, left_ref, coef_ref, stage_ref, sems,
):
    tiles = 4
    rank = lu_hbm.shape[1]
    block = degree_ref.shape[1]
    size = stage_ref.shape[0] // tiles
    degree_copy = start(degree_hbm, degree_ref, sems.at[0])
    sides = [
        start(far_hbm, left_ref.at[:, pl.ds(0, 2 * rank)], sems.at[1]),
        start(lu_hbm, left_ref.at[:, pl.ds(2 * rank, rank)], sems.at[2]),
        start(ll_hbm, left_ref.at[:, pl.ds(3 * rank, rank)], sems.at[3]),
    ]
    copies = load_tiles(base_hbm, stage_ref, tiles, sems, 4)
    parts, height, _ = upper_ref.shape
    lines = rank // parts
    width = (height - lines) // 3
    cols = parts * width
    whole = upper_ref[...]
    own_first = whole[:, :width].reshape(cols, rank)
    first = whole[:, width : 2 * width].reshape(cols, rank)
    second = whole[:, 2 * width : 3 * width].reshape(cols, rank)
    across = whole[:, 3 * width :].reshape(rank, rank)
    second = second + dot(own_first.astype(BF16), (DAMPING * across).astype(BF16))
    down = (DAMPING * low_ref[cols:, :]).astype(BF16)
    lower = (
        low_ref[:cols, :]
        + dot(first.astype(BF16), down[:rank])
        + dot(own_ref[...].astype(BF16), down[rank:])
    )
    coef_ref[:, 0 * rank : 1 * rank] = (DAMPING * first).astype(BF16)
    coef_ref[:, 1 * rank : 2 * rank] = (DAMPING * sib_ref[...]).astype(BF16)
    coef_ref[:, 2 * rank : 3 * rank] = (DAMPING * second).astype(BF16)
    coef_ref[:, 3 * rank : 4 * rank] = (DAMPING * lower).astype(BF16)
    degree_copy.wait()
    columns = degree_columns(degree_ref)
    for side in sides:
        side.wait()
    outs = []
    for tile in range(tiles):
        rows = slice(tile * size, (tile + 1) * size)
        near = pl.ds(tile * size, size)
        product = lax.dot_general(
            left_ref[rows, :], coef_ref[...], (((1,), (1,)), ((), ())), preferred_element_type=F32
        )
        copies[tile].wait()
        stage_ref[rows, :] = stage_ref[rows, :] + scale_tile(
            columns, tile * size // block, product
        )
        outs.append(start(stage_ref.at[near], out_hbm.at[near], sems.at[4 + tile]))
    for out in outs:
        out.wait()


def partner(value, axis, bit):
    pairs = [(source, source ^ (1 << bit)) for source in range(lax.axis_size(axis))]
    return lax.ppermute(value, axis, pairs)


def body(
    queries,
    inv_sqrt_degree,
    leaf_blocks,
    block_cols,
    left_upper,
    right_upper,
    left_lower,
    right_lower,
):
    inner_bits = lax.axis_size("inner").bit_length() - 1
    parts = lax.axis_size("inner") * lax.axis_size("mid")
    rows, cols = queries.shape
    rank = left_upper.shape[1]
    leaves, stored, block, _ = leaf_blocks.shape
    degree = inv_sqrt_degree.reshape(leaves, block)
    width, lines = cols // parts, rank // parts
    height = 2 * width + lines
    dma = pltpu.SemaphoreType.DMA
    degree_scratch = pltpu.VMEM((leaves, block), F32)

    def scratch(*dims):
        return pltpu.VMEM(dims, BF16)

    spread, right, late, early = call(
        coupling_kernel,
        [(degree, FAR), (left_upper, FAR), (left_lower, FAR), (right_upper, FAR), (right_lower, FAR)],
        [
            shape((rows, 2 * rank), BF16),
            shape((rows, 2 * rank), BF16),
            shape((3 * rank, rank), F32),
            shape((rank, rank), F32, True),
        ],
        [degree_scratch]
        + [scratch(rows, rank)] * 4
        + [scratch(rows, 2 * rank)] * 2
        + [pltpu.VMEM((3 * rank, rank), F32), dma((8,))],
        12,
        8 * rows * rank * rank,
    )
    for bit in range(inner_bits - 1):
        early = early + partner(early, "inner", bit)
    cross = partner(early, "inner", inner_bits - 1)

    scaled, coef, first_lower = call(
        first_kernel,
        [(degree, FAR), (queries, FAR), (right_upper, FAR), (right_lower, FAR)],
        [
            shape((rows, cols), BF16),
            shape((cols, 2 * rank), F32),
            shape((cols, rank), F32, True),
        ],
        [degree_scratch, scratch(rows, cols), scratch(rows, 2 * rank), scratch(rows, cols)]
        + [pltpu.VMEM((cols, 2 * rank), F32), dma((11,))],
        12,
        4 * rows * cols * rank,
    )
    own_lower = first_lower
    for bit in range(inner_bits - 1):
        own_lower = own_lower + partner(own_lower, "inner", bit)
    sib_lower = partner(own_lower, "inner", inner_bits - 1)

    dense, low, both = call(
        dense_kernel,
        [(block_cols, SMEM), (leaf_blocks, FAR), (scaled, FAR), (right, FAR), (coef, FAR), (late, FAR), (cross, VMEM)],
        [
            shape((rows, rows), BF16),
            shape((cols + 2 * rank, rank), F32),
            shape((parts, height, rank), F32, True),
        ],
        [scratch(leaves, stored, block, block), scratch(rows, rows), scratch(rows, cols), scratch(rows, 2 * rank)]
        + [pltpu.VMEM((cols, 2 * rank), F32), pltpu.VMEM((3 * rank, rank), F32)]
        + [pltpu.VMEM((cols + 2 * rank, rank), F32), dma((leaves + 4,))],
        36,
        4 * rows * rows * rank,
    )
    both = lax.all_to_all(both, ("mid", "inner"), 0, 0, tiled=True)

    known, far = call(
        known_kernel,
        [(degree, FAR), (dense, FAR), (scaled, FAR), (spread, FAR), (queries, FAR)],
        [shape((rows, cols), BF16), shape((rows, 2 * rank), BF16)],
        [degree_scratch, scratch(rows, rows), scratch(rows, cols), scratch(rows, 2 * rank)]
        + [scratch(rows, cols), scratch(rows, cols), scratch(rows, 2 * rank), dma((16,))],
        28,
        2 * rows * rows * (cols + 2 * rank),
    )
    both, known, far = lax.optimization_barrier((both, known, far))
    both = both.sum(axis=0)
    received = partner(both, "node", 0)
    sib = jnp.concatenate([both[:width], received], axis=0)
    sib = jnp.broadcast_to(sib[None], (parts,) + sib.shape)
    sib = lax.all_to_all(sib, ("mid", "inner"), 0, 0, tiled=True)

    for bit in range(inner_bits - 1):
        low = low + partner(low, "inner", bit)
    low = partner(low, "inner", inner_bits - 1)

    received, known = lax.optimization_barrier((received, known))
    (base,) = call(
        base_kernel,
        [(degree, FAR), (dense, FAR), (known, FAR), (queries, FAR)],
        [shape((rows, cols), F32)],
        [degree_scratch, scratch(rows, rows), scratch(rows, cols), scratch(rows, cols)]
        + [pltpu.VMEM((rows, cols), F32), dma((11,))],
        28,
        2 * rows * rows * cols,
    )

    (out,) = call(
        final_kernel,
        [(degree, FAR), (base, FAR), (far, FAR), (left_upper, FAR), (left_lower, FAR)]
        + [(sib, VMEM), (own_lower, VMEM), (sib_lower, VMEM), (low, VMEM)],
        [shape((rows, cols), F32)],
        [degree_scratch, scratch(rows, 4 * rank), scratch(cols, 4 * rank)]
        + [pltpu.VMEM((rows, cols), F32), dma((8,))],
        20,
        8 * rows * cols * rank,
    )
    return out


def solution(mesh):
    outer, inner = mesh.devices.shape
    fine = Mesh(mesh.devices.reshape(2, outer // 2, inner), ("node", "mid", "inner"))
    rows = P(("node", "mid", "inner"))
    return jax.shard_map(
        body, mesh=fine, in_specs=(rows,) * 8, out_specs=rows, check_vma=False
    )
```

```python
import jax
import jax.numpy as jnp
from jax import lax
from jax.experimental import pallas as pl
from jax.experimental.pallas import tpu as pltpu
from jax.sharding import Mesh
from jax.sharding import PartitionSpec as P

DAMPING = 0.9
F32 = jnp.float32
BF16 = jnp.bfloat16
VMEM = pl.BlockSpec(memory_space=pltpu.VMEM)
SMEM = pl.BlockSpec(memory_space=pltpu.SMEM)
FAR = pl.BlockSpec(memory_space=pltpu.HBM)


def shape(dims, dtype, near=False):
    return (pltpu.VMEM if near else pltpu.HBM)(dims, dtype)


def call(kernel, args, outs, scratch, megabytes, flops):
    values = [
        value if spec is SMEM else pltpu.with_memory_space_constraint(value, spec.memory_space)
        for value, spec in args
    ]
    return pl.pallas_call(
        kernel,
        out_shape=[out for out in outs],
        in_specs=[spec for _, spec in args],
        out_specs=[
            FAR if out.memory_space == pltpu.HBM else VMEM for out in outs
        ],
        scratch_shapes=scratch,
        cost_estimate=pl.CostEstimate(
            flops=flops, bytes_accessed=2**20, transcendentals=0
        ),
        compiler_params=pltpu.CompilerParams(vmem_limit_bytes=megabytes * 2**20),
    )(*values)


def dot(a, b):
    return jnp.dot(a, b, preferred_element_type=F32)


def tdot(a, b):
    return lax.dot_general(a, b, (((0,), (0,)), ((), ())), preferred_element_type=F32)


def start(source, target, sem):
    copy = pltpu.make_async_copy(source, target, sem)
    copy.start()
    return copy


def degree_columns(degree_ref):
    leaves, block = degree_ref.shape
    tall = jnp.concatenate([degree_ref[...]] * (block // leaves), axis=0)
    return tall.T[:, :leaves]


def scale_tile(columns, first, value):
    block = columns.shape[0]
    return jnp.concatenate(
        [
            columns[:, first + b : first + b + 1] * value[b * block : (b + 1) * block]
            for b in range(value.shape[0] // block)
        ],
        axis=0,
    )


def first_kernel(
    degree_hbm, y_hbm, lu_hbm, ll_hbm, ru_hbm, rl_hbm,
    coef_hbm, coupling_hbm, lower_ref,
    degree_ref, y_ref, left_ref, right_ref, scaled_ref, spread_ref, coef_ref, coupling_ref, sems,
):
    leaves, block = degree_ref.shape
    rank = ru_hbm.shape[1]
    upper, lower = pl.ds(0, rank), pl.ds(rank, rank)
    copies = [start(degree_hbm, degree_ref, sems.at[0])]
    for i, (a, b) in enumerate(
        (
            (ll_hbm, left_ref.at[:, lower]),
            (ru_hbm, right_ref.at[:, upper]),
            (rl_hbm, right_ref.at[:, lower]),
            (lu_hbm, left_ref.at[:, upper]),
        )
    ):
        copies.append(start(a, b, sems.at[1 + i]))
    tiles = 4
    loads = load_tiles(y_hbm, y_ref, tiles, sems, 5)
    size = y_ref.shape[0] // tiles
    for copy in copies:
        copy.wait()
    columns = degree_columns(degree_ref)
    square = columns * columns
    for leaf in range(leaves):
        rows = slice(leaf * block, (leaf + 1) * block)
        spread_ref[rows, :] = scale_tile(square, leaf, left_ref[rows, :].astype(F32)).astype(BF16)
    coupling_ref[...] = tdot(spread_ref[...], right_ref[...])
    outs = [start(coupling_ref, coupling_hbm, sems.at[0])]
    for tile in range(tiles):
        loads[tile].wait()
        rows = slice(tile * size, (tile + 1) * size)
        value = y_ref[rows, :].astype(F32)
        scaled_ref[rows, :] = scale_tile(columns, tile * size // block, value).astype(BF16)
    coef_ref[...] = tdot(scaled_ref[...], right_ref[...])
    outs.append(start(coef_ref, coef_hbm, sems.at[1]))
    for slot in range(lower_ref.shape[0]):
        lower_ref[slot] = coef_ref[:, rank:]
    for out in outs:
        out.wait()


def load_tiles(hbm, ref, tiles, sems, first):
    size = ref.shape[0] // tiles
    return [
        start(hbm.at[pl.ds(t * size, size)], ref.at[pl.ds(t * size, size)], sems.at[first + t])
        for t in range(tiles)
    ]


def load_blocks(blocks_hbm, blocks_ref, sems, first):
    return [
        start(blocks_hbm.at[row], blocks_ref.at[row], sems.at[first + row])
        for row in range(blocks_ref.shape[0])
    ]


def place(cols_ref, copies, blocks_ref, dense_ref):
    leaves, stored, block, _ = blocks_ref.shape
    for row in range(leaves):
        rows = slice(row * block, (row + 1) * block)
        dense_ref[rows, :] = jnp.zeros((block, leaves * block), BF16)
        copies[row].wait()
        for j in range(stored):
            col = pl.multiple_of(cols_ref[row, j] * block, block)
            dense_ref[rows, pl.ds(col, block)] = blocks_ref[row, j]


def known_kernel(
    cols_ref, degree_hbm, blocks_hbm, y_hbm, ru_hbm, rl_hbm, coef_hbm, coupling_hbm,
    known_hbm, both_ref, low_ref, lower_coupling_ref,
    degree_ref, blocks_ref, dense_ref, y_ref, scaled_ref, known_ref, right_ref, coef_ref, coupling_ref, sems,
):
    leaves, _, block, _ = blocks_ref.shape
    rank = ru_hbm.shape[1]
    tiles = 4
    size = y_ref.shape[0] // tiles
    degree_copy = start(degree_hbm, degree_ref, sems.at[leaves])
    loads = load_tiles(y_hbm, y_ref, tiles, sems, leaves + 1)
    copies = load_blocks(blocks_hbm, blocks_ref, sems, 0)
    sides = [
        start(ru_hbm, right_ref.at[:, pl.ds(0, rank)], sems.at[leaves + 5]),
        start(rl_hbm, right_ref.at[:, pl.ds(rank, rank)], sems.at[leaves + 6]),
        start(coef_hbm, coef_ref, sems.at[leaves + 7]),
        start(coupling_hbm, coupling_ref, sems.at[leaves + 8]),
    ]
    place(cols_ref, copies, blocks_ref, dense_ref)
    degree_copy.wait()
    columns = degree_columns(degree_ref)
    for tile in range(tiles):
        loads[tile].wait()
        rows = slice(tile * size, (tile + 1) * size)
        value = y_ref[rows, :].astype(F32)
        scaled_ref[rows, :] = scale_tile(columns, tile * size // block, value).astype(BF16)
    for side in sides:
        side.wait()
    outs = []
    for tile in range(tiles):
        rows = slice(tile * size, (tile + 1) * size)
        near = pl.ds(tile * size, size)
        first = tile * size // block
        product = dot(dense_ref[rows, :], scaled_ref[...])
        value = y_ref[rows, :].astype(F32) + DAMPING * scale_tile(columns, first, product)
        known_ref[rows, :] = scale_tile(columns, first, value).astype(BF16)
        outs.append(start(known_ref.at[near], known_hbm.at[near], sems.at[tile]))
    found = tdot(known_ref[...], right_ref[...])
    low_ref[: found.shape[0], :] = found[:, rank:]
    low_ref[found.shape[0] :, :] = coupling_ref[:rank, rank:]
    lower_coupling_ref[...] = coupling_ref[rank:, :]
    parts, height, _ = both_ref.shape
    width = found.shape[0] // parts
    lines = rank // parts
    both_ref[:, :width, :] = coef_ref[:, :rank].reshape(parts, width, rank)
    both_ref[:, width : 2 * width, :] = found[:, :rank].reshape(parts, width, rank)
    for part in range(parts):
        both_ref[part, 2 * width : 2 * width + lines, :] = coupling_ref[
            part * lines : (part + 1) * lines, :rank
        ]
    for out in outs:
        out.wait()


def pack_kernel(
    half_ref, gathered_ref, both_in_ref, low_in_ref, coupling_ref,
    both_ref, low_ref, sib_hbm,
    sib_ref, sem,
):
    count = gathered_ref.shape[0] // 2
    first = (1 - half_ref[0]) * count
    sib = gathered_ref[first]
    for i in range(1, count):
        sib = sib + gathered_ref[first + i]
    sib_ref[...] = sib
    out = start(sib_ref, sib_hbm, sem)
    cols, rank = sib.shape
    update = dot((DAMPING * sib).astype(BF16), coupling_ref[...].astype(BF16))
    parts, height, _ = both_ref.shape
    width = cols // parts
    both_ref[...] = both_in_ref[...]
    both_ref[:, width : 2 * width, :] = both_in_ref[:, width : 2 * width, :] + update[
        :, :rank
    ].reshape(parts, width, rank)
    low_ref[:cols, :] = low_in_ref[:cols, :] + update[:, rank:]
    low_ref[cols:, :] = low_in_ref[cols:, :]
    out.wait()


def far_kernel(
    cols_ref, degree_hbm, blocks_hbm, lu_hbm, ll_hbm,
    far_hbm,
    degree_ref, blocks_ref, dense_ref, left_ref, spread_ref, far_ref, sems,
):
    leaves, _, block, _ = blocks_ref.shape
    rank = lu_hbm.shape[1]
    sides = [
        start(degree_hbm, degree_ref, sems.at[leaves]),
        start(lu_hbm, left_ref.at[:, pl.ds(0, rank)], sems.at[leaves + 1]),
        start(ll_hbm, left_ref.at[:, pl.ds(rank, rank)], sems.at[leaves + 2]),
    ]
    copies = load_blocks(blocks_hbm, blocks_ref, sems, 0)
    for side in sides:
        side.wait()
    columns = degree_columns(degree_ref)
    square = columns * columns
    for leaf in range(leaves):
        rows = slice(leaf * block, (leaf + 1) * block)
        spread_ref[rows, :] = scale_tile(square, leaf, left_ref[rows, :].astype(F32)).astype(BF16)
    place(cols_ref, copies, blocks_ref, dense_ref)
    far_ref[...] = (DAMPING * dot(dense_ref[...], spread_ref[...])).astype(BF16)
    start(far_ref, far_hbm, sems.at[0]).wait()


def base_kernel(
    cols_ref, degree_hbm, blocks_hbm, known_hbm, y_hbm,
    base_hbm,
    degree_ref, blocks_ref, dense_ref, known_ref, y_ref, base_ref, sems,
):
    leaves, _, block, _ = blocks_ref.shape
    copies = load_blocks(blocks_hbm, blocks_ref, sems, 0)
    sides = [
        start(a, b, sems.at[leaves + i])
        for i, (a, b) in enumerate(
            ((degree_hbm, degree_ref), (known_hbm, known_ref), (y_hbm, y_ref))
        )
    ]
    place(cols_ref, copies, blocks_ref, dense_ref)
    for side in sides:
        side.wait()
    columns = degree_columns(degree_ref)
    tiles = 4
    size = y_ref.shape[0] // tiles
    outs = []
    for tile in range(tiles):
        rows = slice(tile * size, (tile + 1) * size)
        near = pl.ds(tile * size, size)
        product = dot(dense_ref[rows, :], known_ref[...])
        base_ref[rows, :] = y_ref[rows, :].astype(F32) + DAMPING * scale_tile(
            columns, tile * size // block, product
        )
        outs.append(start(base_ref.at[near], base_hbm.at[near], sems.at[tile]))
    for out in outs:
        out.wait()


def final_kernel(
    degree_hbm, base_hbm, far_hbm, lu_hbm, ll_hbm, sib_hbm, upper_ref, low_ref,
    out_hbm,
    degree_ref, left_ref, coef_ref, sib_ref, stage_ref, sems,
):
    tiles = 4
    rank = lu_hbm.shape[1]
    block = degree_ref.shape[1]
    size = stage_ref.shape[0] // tiles
    degree_copy = start(degree_hbm, degree_ref, sems.at[0])
    sib_copy = start(sib_hbm, sib_ref, sems.at[8])
    sides = [
        start(far_hbm, left_ref.at[:, pl.ds(0, 2 * rank)], sems.at[1]),
        start(lu_hbm, left_ref.at[:, pl.ds(2 * rank, rank)], sems.at[2]),
        start(ll_hbm, left_ref.at[:, pl.ds(3 * rank, rank)], sems.at[3]),
    ]
    copies = load_tiles(base_hbm, stage_ref, tiles, sems, 4)
    parts, height, _ = upper_ref.shape
    lines = rank // parts
    width = (height - lines) // 3
    cols = parts * width
    whole = upper_ref[...]
    own_first = whole[:, :width].reshape(cols, rank)
    first = whole[:, width : 2 * width].reshape(cols, rank)
    second = whole[:, 2 * width : 3 * width].reshape(cols, rank)
    across = whole[:, 3 * width :].reshape(rank, rank)
    second = second + dot(own_first.astype(BF16), (DAMPING * across).astype(BF16))
    down = (DAMPING * low_ref[cols:, :]).astype(BF16)
    lower = low_ref[:cols, :] + dot(first.astype(BF16), down)
    sib_copy.wait()
    coef_ref[:, 0 * rank : 1 * rank] = (DAMPING * first).astype(BF16)
    coef_ref[:, 1 * rank : 2 * rank] = (DAMPING * sib_ref[...]).astype(BF16)
    coef_ref[:, 2 * rank : 3 * rank] = (DAMPING * second).astype(BF16)
    coef_ref[:, 3 * rank : 4 * rank] = (DAMPING * lower).astype(BF16)
    degree_copy.wait()
    columns = degree_columns(degree_ref)
    for side in sides:
        side.wait()
    outs = []
    for tile in range(tiles):
        rows = slice(tile * size, (tile + 1) * size)
        near = pl.ds(tile * size, size)
        product = lax.dot_general(
            left_ref[rows, :], coef_ref[...], (((1,), (1,)), ((), ())), preferred_element_type=F32
        )
        copies[tile].wait()
        stage_ref[rows, :] = stage_ref[rows, :] + scale_tile(
            columns, tile * size // block, product
        )
        outs.append(start(stage_ref.at[near], out_hbm.at[near], sems.at[4 + tile]))
    for out in outs:
        out.wait()


def partner(value, axis, bit):
    pairs = [(source, source ^ (1 << bit)) for source in range(lax.axis_size(axis))]
    return lax.ppermute(value, axis, pairs)


def body(
    queries,
    inv_sqrt_degree,
    leaf_blocks,
    block_cols,
    left_upper,
    right_upper,
    left_lower,
    right_lower,
):
    inner_bits = lax.axis_size("inner").bit_length() - 1
    parts = lax.axis_size("inner") * lax.axis_size("mid")
    rows, cols = queries.shape
    rank = left_upper.shape[1]
    leaves, stored, block, _ = leaf_blocks.shape
    degree = inv_sqrt_degree.reshape(leaves, block)
    width, lines = cols // parts, rank // parts
    height = 2 * width + lines
    dma = pltpu.SemaphoreType.DMA
    degree_scratch = pltpu.VMEM((leaves, block), F32)

    def scratch(*dims):
        return pltpu.VMEM(dims, BF16)

    near_f32 = lambda *dims: pltpu.VMEM(dims, F32)
    inner = lax.axis_size("inner")
    coef, coupling, gathered = call(
        first_kernel,
        [(degree, FAR), (queries, FAR), (left_upper, FAR), (left_lower, FAR), (right_upper, FAR), (right_lower, FAR)],
        [
            shape((cols, 2 * rank), F32),
            shape((2 * rank, 2 * rank), F32),
            shape((inner, cols, rank), F32, True),
        ],
        [degree_scratch, scratch(rows, cols), scratch(rows, 2 * rank), scratch(rows, 2 * rank)]
        + [scratch(rows, cols), scratch(rows, 2 * rank), near_f32(cols, 2 * rank)]
        + [near_f32(2 * rank, 2 * rank), dma((9,))],
        14,
        4 * rows * (cols + 2 * rank) * rank,
    )
    gathered = lax.all_to_all(gathered, "inner", 0, 0, tiled=True)

    known, both, low, lower_coupling = call(
        known_kernel,
        [(block_cols, SMEM), (degree, FAR), (leaf_blocks, FAR), (queries, FAR), (right_upper, FAR), (right_lower, FAR)]
        + [(coef, FAR), (coupling, FAR)],
        [
            shape((rows, cols), BF16),
            shape((parts, height, rank), F32, True),
            shape((cols + rank, rank), F32, True),
            shape((rank, 2 * rank), F32, True),
        ],
        [degree_scratch, scratch(leaves, stored, block, block), scratch(rows, rows), scratch(rows, cols)]
        + [scratch(rows, cols), scratch(rows, cols), scratch(rows, 2 * rank), near_f32(cols, 2 * rank)]
        + [near_f32(2 * rank, 2 * rank), dma((leaves + 9,))],
        36,
        2 * rows * rows * cols,
    )
    half = (lax.axis_index("inner") // (inner // 2)).astype(jnp.int32).reshape(1)
    both, low, sib_lower = call(
        pack_kernel,
        [(half, SMEM), (gathered, VMEM), (both, VMEM), (low, VMEM), (lower_coupling, VMEM)],
        [
            shape((parts, height, rank), F32, True),
            shape((cols + rank, rank), F32, True),
            shape((cols, rank), F32),
        ],
        [near_f32(cols, rank), dma(())],
        8,
        4 * cols * rank * rank,
    )
    both = lax.all_to_all(both, ("mid", "inner"), 0, 0, tiled=True)

    (far,) = call(
        far_kernel,
        [(block_cols, SMEM), (degree, FAR), (leaf_blocks, FAR), (left_upper, FAR), (left_lower, FAR)],
        [shape((rows, 2 * rank), BF16)],
        [degree_scratch, scratch(leaves, stored, block, block), scratch(rows, rows)]
        + [scratch(rows, 2 * rank)] * 3
        + [dma((leaves + 3,))],
        26,
        4 * rows * rows * rank,
    )
    both, far = lax.optimization_barrier((both, far))
    both = both.sum(axis=0)
    received = partner(both, "node", 0)
    for bit in range(inner_bits - 1):
        low = low + partner(low, "inner", bit)
    received, low, known = lax.optimization_barrier((received, low, known))
    low = partner(low, "inner", inner_bits - 1)
    sib = jnp.concatenate([both[:width], received], axis=0)
    sib = jnp.broadcast_to(sib[None], (parts,) + sib.shape)
    sib = lax.all_to_all(sib, ("mid", "inner"), 0, 0, tiled=True)


    (base,) = call(
        base_kernel,
        [(block_cols, SMEM), (degree, FAR), (leaf_blocks, FAR), (known, FAR), (queries, FAR)],
        [shape((rows, cols), F32)],
        [degree_scratch, scratch(leaves, stored, block, block), scratch(rows, rows)]
        + [scratch(rows, cols)] * 2
        + [near_f32(rows, cols), dma((leaves + 3,))],
        32,
        2 * rows * rows * cols,
    )

    (out,) = call(
        final_kernel,
        [(degree, FAR), (base, FAR), (far, FAR), (left_upper, FAR), (left_lower, FAR)]
        + [(sib_lower, FAR), (sib, VMEM), (low, VMEM)],
        [shape((rows, cols), F32)],
        [degree_scratch, scratch(rows, 4 * rank), scratch(cols, 4 * rank)]
        + [near_f32(cols, rank), near_f32(rows, cols), dma((9,))],
        20,
        8 * rows * cols * rank,
    )
    return out


def solution(mesh):
    outer, inner = mesh.devices.shape
    fine = Mesh(mesh.devices.reshape(2, outer // 2, inner), ("node", "mid", "inner"))
    rows = P(("node", "mid", "inner"))
    return jax.shard_map(
        body, mesh=fine, in_specs=(rows,) * 8, out_specs=rows, check_vma=False
    )
```

```python
import functools

import jax
import jax.numpy as jnp
from jax import lax
from jax.experimental import pallas as pl
from jax.experimental.pallas import tpu as pltpu
from jax.sharding import Mesh
from jax.sharding import PartitionSpec as P

DAMPING = 0.9
F32 = jnp.float32
BF16 = jnp.bfloat16
VMEM = pl.BlockSpec(memory_space=pltpu.VMEM)
SMEM = pl.BlockSpec(memory_space=pltpu.SMEM)
FAR = pl.BlockSpec(memory_space=pltpu.HBM)


def shape(dims, dtype, near=False):
    return (pltpu.VMEM if near else pltpu.HBM)(dims, dtype)


def call(kernel, args, outs, scratch, megabytes, flops):
    values = [
        value if spec is SMEM else pltpu.with_memory_space_constraint(value, spec.memory_space)
        for value, spec in args
    ]
    return pl.pallas_call(
        kernel,
        out_shape=[out for out in outs],
        in_specs=[spec for _, spec in args],
        out_specs=[
            FAR if out.memory_space == pltpu.HBM else VMEM for out in outs
        ],
        scratch_shapes=scratch,
        cost_estimate=pl.CostEstimate(
            flops=flops, bytes_accessed=2**20, transcendentals=0
        ),
        compiler_params=pltpu.CompilerParams(vmem_limit_bytes=megabytes * 2**20),
    )(*values)


def dot(a, b):
    return jnp.dot(a, b, preferred_element_type=F32)


def tdot(a, b):
    return lax.dot_general(a, b, (((0,), (0,)), ((), ())), preferred_element_type=F32)


def start(source, target, sem):
    copy = pltpu.make_async_copy(source, target, sem)
    copy.start()
    return copy


def degree_columns(degree_ref):
    leaves, block = degree_ref.shape
    tall = jnp.concatenate([degree_ref[...]] * (block // leaves), axis=0)
    return tall.T[:, :leaves]


def scale_tile(columns, first, value):
    block = columns.shape[0]
    return jnp.concatenate(
        [
            columns[:, first + b : first + b + 1] * value[b * block : (b + 1) * block]
            for b in range(value.shape[0] // block)
        ],
        axis=0,
    )


def load_tiles(hbm, ref, tiles, sems, first):
    size = ref.shape[0] // tiles
    return [
        start(hbm.at[pl.ds(t * size, size)], ref.at[pl.ds(t * size, size)], sems.at[first + t])
        for t in range(tiles)
    ]


def first_kernel(
    degree_hbm, y_hbm, rl_hbm,
    lower_ref,
    degree_ref, y_ref, right_ref, scaled_ref, sems,
):
    block = degree_ref.shape[1]
    tiles = 4
    size = y_ref.shape[0] // tiles
    degree_copy = start(degree_hbm, degree_ref, sems.at[tiles])
    right_copy = start(rl_hbm, right_ref, sems.at[tiles + 1])
    loads = load_tiles(y_hbm, y_ref, tiles, sems, 0)
    degree_copy.wait()
    columns = degree_columns(degree_ref)
    right_copy.wait()
    for tile in range(tiles):
        loads[tile].wait()
        rows = slice(tile * size, (tile + 1) * size)
        value = y_ref[rows, :].astype(F32)
        scaled_ref[rows, :] = scale_tile(columns, tile * size // block, value).astype(BF16)
    lower_ref[...] = tdot(scaled_ref[...], right_ref[...])


def place(cols_ref, blocks_ref, dense_ref):
    leaves, stored, block, _ = blocks_ref.shape
    for row in range(leaves):
        rows = slice(row * block, (row + 1) * block)
        dense_ref[rows, :] = jnp.zeros((block, leaves * block), BF16)
        for j in range(stored):
            col = pl.multiple_of(cols_ref[row, j] * block, block)
            dense_ref[rows, pl.ds(col, block)] = blocks_ref[row, j]


def known_kernel(
    cols_hbm, degree_hbm, blocks_hbm, y_hbm, lu_hbm, ll_hbm, ru_hbm, rl_hbm,
    known_hbm, dense_hbm, both_ref, low_ref, lower_coupling_ref,
    cols_ref, degree_ref, blocks_ref, dense_ref, y_ref, scaled_ref, known_ref, left_ref, spread_ref, right_ref, sems,
):
    leaves, _, block, _ = blocks_ref.shape
    rank = ru_hbm.shape[1]
    sides = [
        start(a, b, sems.at[i])
        for i, (a, b) in enumerate(
            (
                (degree_hbm, degree_ref),
                (cols_hbm, cols_ref),
                (lu_hbm, left_ref.at[:, pl.ds(0, rank)]),
                (ll_hbm, left_ref.at[:, pl.ds(rank, rank)]),
                (ru_hbm, right_ref.at[:, pl.ds(0, rank)]),
                (rl_hbm, right_ref.at[:, pl.ds(rank, rank)]),
                (y_hbm, y_ref),
            )
        )
    ]
    sides[0].wait()
    columns = degree_columns(degree_ref)
    square = columns * columns
    loads = load_tiles(blocks_hbm, blocks_ref, 4, sems, 7)
    for side in sides[1:]:
        side.wait()
    for leaf in range(leaves):
        rows = slice(leaf * block, (leaf + 1) * block)
        spread_ref[rows, :] = scale_tile(square, leaf, left_ref[rows, :].astype(F32)).astype(BF16)
        scaled_ref[rows, :] = scale_tile(columns, leaf, y_ref[rows, :].astype(F32)).astype(BF16)
    coupling = tdot(spread_ref[...], right_ref[...])
    parts, height, _ = both_ref.shape
    cols = scaled_ref.shape[1]
    width = cols // parts
    lines = rank // parts
    both_ref[:, :width, :] = tdot(scaled_ref[...], right_ref[:, :rank]).reshape(parts, width, rank)
    both_ref[:, 2 * width :, :] = coupling[:rank, :rank].reshape(parts, lines, rank)
    low_ref[cols:, :] = coupling[:rank, rank:]
    lower_coupling_ref[...] = coupling[rank:, :]
    for load in loads:
        load.wait()
    place(cols_ref, blocks_ref, dense_ref)
    outs = [start(dense_ref, dense_hbm, sems.at[0])]
    tiles = 4
    size = y_ref.shape[0] // tiles
    for tile in range(tiles):
        rows = slice(tile * size, (tile + 1) * size)
        first = tile * size // block
        product = dot(dense_ref[rows, :], scaled_ref[...])
        value = y_ref[rows, :].astype(F32) + DAMPING * scale_tile(columns, first, product)
        known_ref[rows, :] = scale_tile(columns, first, value).astype(BF16)
    outs.append(start(known_ref, known_hbm, sems.at[1]))
    found = tdot(known_ref[...], right_ref[...])
    low_ref[:cols, :] = found[:, rank:]
    both_ref[:, width : 2 * width, :] = found[:, :rank].reshape(parts, width, rank)
    for out in outs:
        out.wait()


def pack_kernel(*refs):
    both_in_ref, low_in_ref, coupling_ref = refs[:3]
    received = refs[3:-6]
    both_ref, low_a_ref, low_b_ref, sib_hbm, sib_ref, sem = refs[-6:]
    sib = received[0][...]
    for other in received[1:]:
        sib = sib + other[...]
    sib_ref[...] = sib
    out = start(sib_ref, sib_hbm, sem)
    cols, rank = sib.shape
    update = dot((DAMPING * sib).astype(BF16), coupling_ref[...].astype(BF16))
    parts, height, _ = both_ref.shape
    width = cols // parts
    both_ref[:, :width, :] = both_in_ref[:, :width, :]
    both_ref[:, 2 * width :, :] = both_in_ref[:, 2 * width :, :]
    both_ref[:, width : 2 * width, :] = both_in_ref[:, width : 2 * width, :] + update[
        :, :rank
    ].reshape(parts, width, rank)
    half = low_a_ref.shape[0]
    low_a_ref[...] = low_in_ref[:half, :] + update[:half, rank:]
    low_b_ref[: cols - half, :] = low_in_ref[half:cols, :] + update[half:, rank:]
    low_b_ref[cols - half :, :] = low_in_ref[cols:, :]
    out.wait()


def far_kernel(
    degree_hbm, dense_hbm, lu_hbm, ll_hbm,
    far_hbm,
    degree_ref, dense_ref, left_ref, spread_ref, far_ref, sems,
):
    leaves, block = degree_ref.shape
    rank = lu_hbm.shape[1]
    tiles = 4
    sides = [
        start(degree_hbm, degree_ref, sems.at[tiles]),
        start(lu_hbm, left_ref.at[:, pl.ds(0, rank)], sems.at[tiles + 1]),
        start(ll_hbm, left_ref.at[:, pl.ds(rank, rank)], sems.at[tiles + 2]),
    ]
    copies = load_tiles(dense_hbm, dense_ref, tiles, sems, 0)
    for side in sides:
        side.wait()
    columns = degree_columns(degree_ref)
    square = columns * columns
    for leaf in range(leaves):
        rows = slice(leaf * block, (leaf + 1) * block)
        spread_ref[rows, :] = scale_tile(square, leaf, left_ref[rows, :].astype(F32)).astype(BF16)
    for copy in copies:
        copy.wait()
    far_ref[...] = (DAMPING * dot(dense_ref[...], spread_ref[...])).astype(BF16)
    start(far_ref, far_hbm, sems.at[0]).wait()


def local_kernel(
    dense_hbm, known_hbm,
    local_hbm,
    dense_ref, known_ref, local_ref, sems,
):
    tiles = 4
    size = dense_ref.shape[0] // tiles
    known_copy = start(known_hbm, known_ref, sems.at[tiles])
    loads = load_tiles(dense_hbm, dense_ref, tiles, sems, 0)
    known_copy.wait()
    for load in loads:
        load.wait()
    outs = []
    for half in range(2):
        rows = slice(half * 2 * size, (half + 1) * 2 * size)
        near = pl.ds(half * 2 * size, 2 * size)
        local_ref[rows, :] = (DAMPING * dot(dense_ref[rows, :], known_ref[...])).astype(BF16)
        outs.append(start(local_ref.at[near], local_hbm.at[near], sems.at[half]))
    for out in outs:
        out.wait()


def final_kernel(
    inner, core_ref, degree_hbm, far_hbm, lu_hbm, ll_hbm, sib_hbm, y_hbm, local_hbm, mine_ref, other_ref, low_a_ref, low_b_ref,
    out_hbm,
    degree_ref, left_ref, coef_ref, sib_ref, own_ref, first_ref, second_ref, across_ref, low_ref, y_ref, local_ref, stage_ref, sems,
):
    tiles = 4
    rank = lu_hbm.shape[1]
    block = degree_ref.shape[1]
    size = stage_ref.shape[0] // tiles
    degree_copy = start(degree_hbm, degree_ref, sems.at[0])
    sib_copy = start(sib_hbm, sib_ref, sems.at[1])
    sides = [
        start(far_hbm, left_ref.at[:, pl.ds(0, 2 * rank)], sems.at[2]),
        start(lu_hbm, left_ref.at[:, pl.ds(2 * rank, rank)], sems.at[3]),
        start(ll_hbm, left_ref.at[:, pl.ds(3 * rank, rank)], sems.at[4]),
    ]
    loads = load_tiles(y_hbm, y_ref, tiles, sems, 5)
    others = load_tiles(local_hbm, local_ref, tiles, sems, 9)
    slots = mine_ref.shape[0]
    cols = own_ref.shape[0]
    width = cols // (2 * slots)
    lines = rank // (2 * slots)
    for source, core in ((mine_ref, core_ref[0]), (other_ref, 1 - core_ref[0])):
        for rest in range(slots // inner):
            some = source[rest * inner : (rest + 1) * inner]
            span = inner * width
            at = pl.ds(pl.multiple_of((2 * rest + core) * span, span), span)
            own_ref[at, :] = some[:, :width].reshape(span, rank)
            first_ref[at, :] = some[:, width : 2 * width].reshape(span, rank)
            second_ref[at, :] = some[:, 2 * width : 3 * width].reshape(span, rank)
            span = inner * lines
            at = pl.ds(pl.multiple_of((2 * rest + core) * span, span), span)
            across_ref[at, :] = some[:, 3 * width :].reshape(span, rank)
    half = low_a_ref.shape[0]
    low_ref[:half, :] = low_a_ref[...]
    low_ref[half:, :] = low_b_ref[...]
    first = first_ref[...]
    second = second_ref[...] + dot(
        own_ref[...].astype(BF16), (DAMPING * across_ref[...]).astype(BF16)
    )
    down = (DAMPING * low_ref[cols:, :]).astype(BF16)
    lower = low_ref[:cols, :] + dot(first.astype(BF16), down)
    sib_copy.wait()
    coef_ref[:, 0 * rank : 1 * rank] = (DAMPING * first).astype(BF16)
    coef_ref[:, 1 * rank : 2 * rank] = (DAMPING * sib_ref[...]).astype(BF16)
    coef_ref[:, 2 * rank : 3 * rank] = (DAMPING * second).astype(BF16)
    coef_ref[:, 3 * rank : 4 * rank] = (DAMPING * lower).astype(BF16)
    degree_copy.wait()
    columns = degree_columns(degree_ref)
    for side in sides:
        side.wait()
    outs = []
    for tile in range(tiles):
        rows = slice(tile * size, (tile + 1) * size)
        near = pl.ds(tile * size, size)
        product = lax.dot_general(
            left_ref[rows, :], coef_ref[...], (((1,), (1,)), ((), ())), preferred_element_type=F32
        )
        loads[tile].wait()
        others[tile].wait()
        stage_ref[rows, :] = y_ref[rows, :].astype(F32) + scale_tile(
            columns, tile * size // block, local_ref[rows, :].astype(F32) + product
        )
        outs.append(start(stage_ref.at[near], out_hbm.at[near], sems.at[tile]))
    for out in outs:
        out.wait()


def partner(value, axis, mask):
    pairs = [(source, source ^ mask) for source in range(lax.axis_size(axis))]
    return lax.ppermute(value, axis, pairs)


def low_bits(axis):
    masks = []
    while 2 ** (len(masks) + 1) < lax.axis_size(axis):
        masks.append(2 ** len(masks))
    return masks


def body(
    queries,
    inv_sqrt_degree,
    leaf_blocks,
    block_cols,
    left_upper,
    right_upper,
    left_lower,
    right_lower,
):
    inner = lax.axis_size("inner")
    parts = inner * lax.axis_size("rest") * lax.axis_size("core")
    rows, cols = queries.shape
    rank = left_upper.shape[1]
    leaves, stored, block, _ = leaf_blocks.shape
    degree = inv_sqrt_degree.reshape(leaves, block)
    width, lines = cols // parts, rank // parts
    height = 2 * width + lines
    node = ("rest", "core", "inner")
    dma = pltpu.SemaphoreType.DMA
    degree_scratch = pltpu.VMEM((leaves, block), F32)

    def scratch(*dims):
        return pltpu.VMEM(dims, BF16)

    def wide(*dims):
        return pltpu.VMEM(dims, F32)

    (first_lower,) = call(
        first_kernel,
        [(degree, FAR), (queries, FAR), (right_lower, FAR)],
        [shape((cols, rank), F32, True)],
        [degree_scratch, scratch(rows, cols), scratch(rows, rank), scratch(rows, cols), dma((6,))],
        8,
        2 * rows * cols * rank,
    )
    first_sib = [
        partner(first_lower, "inner", inner // 2 + other) for other in range(inner // 2)
    ]

    known, dense, both, low, lower_coupling = call(
        known_kernel,
        [(block_cols, FAR), (degree, FAR), (leaf_blocks, FAR), (queries, FAR)]
        + [(left_upper, FAR), (left_lower, FAR), (right_upper, FAR), (right_lower, FAR)],
        [
            shape((rows, cols), BF16),
            shape((rows, rows), BF16),
            shape((parts, height, rank), F32, True),
            shape((cols + rank, rank), F32, True),
            shape((rank, 2 * rank), F32, True),
        ],
        [pltpu.SMEM((leaves, stored), jnp.int32), degree_scratch]
        + [scratch(leaves, stored, block, block), scratch(rows, rows)]
        + [scratch(rows, cols)] * 3
        + [scratch(rows, 2 * rank)] * 3
        + [dma((11,))],
        36,
        2 * rows * rows * cols,
    )
    split = (cols + rank) // 2
    both, low_a, low_b, sib_lower = call(
        pack_kernel,
        [(both, VMEM), (low, VMEM), (lower_coupling, VMEM)] + [(value, VMEM) for value in first_sib],
        [
            shape((parts, height, rank), F32, True),
            shape((split, rank), F32, True),
            shape((cols + rank - split, rank), F32, True),
            shape((cols, rank), F32),
        ],
        [wide(cols, rank), dma(())],
        8,
        4 * cols * rank * rank,
    )
    both = lax.all_to_all(both, node, 0, 0, tiled=True)

    (far,) = call(
        far_kernel,
        [(degree, FAR), (dense, FAR), (left_upper, FAR), (left_lower, FAR)],
        [shape((rows, 2 * rank), BF16)],
        [degree_scratch, scratch(rows, rows)] + [scratch(rows, 2 * rank)] * 3 + [dma((7,))],
        20,
        4 * rows * rows * rank,
    )
    both, far = lax.optimization_barrier((both, far))
    both = both.sum(axis=0)
    received = partner(both, "node", 1)

    for mask in low_bits("inner"):
        low_a = low_a + partner(low_a, "inner", mask)
    low_b = partner(low_b, "inner", inner // 2)

    received, low_a, low_b, known = lax.optimization_barrier((received, low_a, low_b, known))
    sib = jnp.concatenate([both[:width], received], axis=0)
    sib = jnp.broadcast_to(sib[None], (parts // 2,) + sib.shape)
    sib = lax.all_to_all(sib, ("rest", "inner"), 0, 0, tiled=True)
    low_a = partner(low_a, "inner", inner // 2)
    for mask in low_bits("inner"):
        low_b = low_b + partner(low_b, "inner", mask)

    (local,) = call(
        local_kernel,
        [(dense, FAR), (known, FAR)],
        [shape((rows, cols), BF16)],
        [scratch(rows, rows), scratch(rows, cols), scratch(rows, cols), dma((5,))],
        20,
        2 * rows * rows * cols,
    )

    sib, local, low_a, low_b = lax.optimization_barrier((sib, local, low_a, low_b))
    other = partner(sib, "core", 1)
    core = lax.axis_index("core").astype(jnp.int32).reshape(1)
    (out,) = call(
        functools.partial(final_kernel, inner),
        [(core, SMEM), (degree, FAR), (far, FAR), (left_upper, FAR), (left_lower, FAR), (sib_lower, FAR)]
        + [(queries, FAR), (local, FAR), (sib, VMEM), (other, VMEM), (low_a, VMEM), (low_b, VMEM)],
        [shape((rows, cols), F32)],
        [degree_scratch, scratch(rows, 4 * rank), scratch(cols, 4 * rank)]
        + [wide(cols, rank)] * 4
        + [wide(rank, rank), wide(cols + rank, rank), scratch(rows, cols), scratch(rows, cols)]
        + [wide(rows, cols), dma((13,))],
        20,
        8 * rows * cols * rank,
    )
    return out


def solution(mesh):
    outer, inner = mesh.devices.shape
    fine = Mesh(mesh.devices.reshape(2, outer // 4, 2, inner), ("node", "rest", "core", "inner"))
    rows = P(("node", "rest", "core", "inner"))
    return jax.shard_map(
        body, mesh=fine, in_specs=(rows,) * 8, out_specs=rows, check_vma=False
    )
```

```python
import functools

import jax
import jax.numpy as jnp
from jax import lax
from jax.experimental import pallas as pl
from jax.experimental.pallas import tpu as pltpu
from jax.sharding import Mesh
from jax.sharding import PartitionSpec as P

DAMPING = 0.9
F32 = jnp.float32
BF16 = jnp.bfloat16
VMEM = pl.BlockSpec(memory_space=pltpu.VMEM)
SMEM = pl.BlockSpec(memory_space=pltpu.SMEM)
FAR = pl.BlockSpec(memory_space=pltpu.HBM)


def shape(dims, dtype, near=False):
    return (pltpu.VMEM if near else pltpu.HBM)(dims, dtype)


def call(kernel, args, outs, scratch, megabytes, flops):
    values = [
        value if spec is SMEM else pltpu.with_memory_space_constraint(value, spec.memory_space)
        for value, spec in args
    ]
    return pl.pallas_call(
        kernel,
        out_shape=[out for out in outs],
        in_specs=[spec for _, spec in args],
        out_specs=[
            FAR if out.memory_space == pltpu.HBM else VMEM for out in outs
        ],
        scratch_shapes=scratch,
        cost_estimate=pl.CostEstimate(
            flops=flops, bytes_accessed=2**20, transcendentals=0
        ),
        compiler_params=pltpu.CompilerParams(vmem_limit_bytes=megabytes * 2**20),
    )(*values)


def dot(a, b):
    return jnp.dot(a, b, preferred_element_type=F32)


def tdot(a, b):
    return lax.dot_general(a, b, (((0,), (0,)), ((), ())), preferred_element_type=F32)


def start(source, target, sem):
    copy = pltpu.make_async_copy(source, target, sem)
    copy.start()
    return copy


def degree_columns(degree_ref):
    leaves, block = degree_ref.shape
    tall = jnp.concatenate([degree_ref[...]] * (block // leaves), axis=0)
    return tall.T[:, :leaves]


def scale_tile(columns, first, value):
    block = columns.shape[0]
    return jnp.concatenate(
        [
            columns[:, first + b : first + b + 1] * value[b * block : (b + 1) * block]
            for b in range(value.shape[0] // block)
        ],
        axis=0,
    )


def load_tiles(hbm, ref, tiles, sems, first):
    size = ref.shape[0] // tiles
    return [
        start(hbm.at[pl.ds(t * size, size)], ref.at[pl.ds(t * size, size)], sems.at[first + t])
        for t in range(tiles)
    ]


def first_kernel(
    degree_hbm, y_hbm, rl_hbm,
    lower_ref,
    degree_ref, y_ref, right_ref, scaled_ref, sems,
):
    block = degree_ref.shape[1]
    tiles = 4
    size = y_ref.shape[0] // tiles
    degree_copy = start(degree_hbm, degree_ref, sems.at[tiles])
    right_copy = start(rl_hbm, right_ref, sems.at[tiles + 1])
    loads = load_tiles(y_hbm, y_ref, tiles, sems, 0)
    degree_copy.wait()
    columns = degree_columns(degree_ref)
    right_copy.wait()
    for tile in range(tiles):
        loads[tile].wait()
        rows = slice(tile * size, (tile + 1) * size)
        value = y_ref[rows, :].astype(F32)
        scaled_ref[rows, :] = scale_tile(columns, tile * size // block, value).astype(BF16)
    lower_ref[...] = tdot(scaled_ref[...], right_ref[...])


def place(cols_ref, blocks_ref, dense_ref):
    leaves, stored, block, _ = blocks_ref.shape
    for row in range(leaves):
        rows = slice(row * block, (row + 1) * block)
        dense_ref[rows, :] = jnp.zeros((block, leaves * block), BF16)
        for j in range(stored):
            col = pl.multiple_of(cols_ref[row, j] * block, block)
            dense_ref[rows, pl.ds(col, block)] = blocks_ref[row, j]


def known_kernel(
    cols_hbm, degree_hbm, blocks_hbm, y_hbm, lu_hbm, ll_hbm, ru_hbm, rl_hbm,
    known_hbm, dense_hbm, both_ref, low_ref, lower_coupling_ref,
    cols_ref, degree_ref, blocks_ref, dense_ref, y_ref, scaled_ref, known_ref, left_ref, spread_ref, right_ref, sems,
):
    leaves, _, block, _ = blocks_ref.shape
    rank = ru_hbm.shape[1]
    sides = [
        start(a, b, sems.at[i])
        for i, (a, b) in enumerate(
            (
                (degree_hbm, degree_ref),
                (cols_hbm, cols_ref),
                (lu_hbm, left_ref.at[:, pl.ds(0, rank)]),
                (ll_hbm, left_ref.at[:, pl.ds(rank, rank)]),
                (ru_hbm, right_ref.at[:, pl.ds(0, rank)]),
                (rl_hbm, right_ref.at[:, pl.ds(rank, rank)]),
                (y_hbm, y_ref),
            )
        )
    ]
    sides[0].wait()
    columns = degree_columns(degree_ref)
    square = columns * columns
    loads = load_tiles(blocks_hbm, blocks_ref, 4, sems, 7)
    for side in sides[1:]:
        side.wait()
    for leaf in range(leaves):
        rows = slice(leaf * block, (leaf + 1) * block)
        spread_ref[rows, :] = scale_tile(square, leaf, left_ref[rows, :].astype(F32)).astype(BF16)
        scaled_ref[rows, :] = scale_tile(columns, leaf, y_ref[rows, :].astype(F32)).astype(BF16)
    coupling = tdot(spread_ref[...], right_ref[...])
    parts, height, _ = both_ref.shape
    cols = scaled_ref.shape[1]
    width = cols // parts
    lines = rank // parts
    both_ref[:, :width, :] = tdot(scaled_ref[...], right_ref[:, :rank]).reshape(parts, width, rank)
    both_ref[:, 2 * width :, :] = coupling[:rank, :rank].reshape(parts, lines, rank)
    low_ref[cols:, :] = coupling[:rank, rank:]
    lower_coupling_ref[...] = coupling[rank:, :]
    for load in loads:
        load.wait()
    place(cols_ref, blocks_ref, dense_ref)
    outs = [start(dense_ref, dense_hbm, sems.at[0])]
    tiles = 4
    size = y_ref.shape[0] // tiles
    for tile in range(tiles):
        rows = slice(tile * size, (tile + 1) * size)
        first = tile * size // block
        product = dot(dense_ref[rows, :], scaled_ref[...])
        value = y_ref[rows, :].astype(F32) + DAMPING * scale_tile(columns, first, product)
        known_ref[rows, :] = scale_tile(columns, first, value).astype(BF16)
        if tile % 2 == 1:
            near = pl.ds((tile - 1) * size, 2 * size)
            outs.append(start(known_ref.at[near], known_hbm.at[near], sems.at[1 + tile]))
    found = tdot(known_ref[...], right_ref[...])
    low_ref[:cols, :] = found[:, rank:]
    both_ref[:, width : 2 * width, :] = found[:, :rank].reshape(parts, width, rank)
    for out in outs:
        out.wait()


def pack_kernel(*refs):
    both_in_ref, low_in_ref, coupling_ref = refs[:3]
    received = refs[3:-6]
    both_ref, low_a_ref, low_b_ref, sib_hbm, sib_ref, sem = refs[-6:]
    sib = received[0][...]
    for other in received[1:]:
        sib = sib + other[...]
    sib_ref[...] = sib
    out = start(sib_ref, sib_hbm, sem)
    cols, rank = sib.shape
    update = dot((DAMPING * sib).astype(BF16), coupling_ref[...].astype(BF16))
    parts, height, _ = both_ref.shape
    width = cols // parts
    both_ref[:, :width, :] = both_in_ref[:, :width, :]
    both_ref[:, 2 * width :, :] = both_in_ref[:, 2 * width :, :]
    both_ref[:, width : 2 * width, :] = both_in_ref[:, width : 2 * width, :] + update[
        :, :rank
    ].reshape(parts, width, rank)
    half = low_a_ref.shape[0]
    low_a_ref[...] = low_in_ref[:half, :] + update[:half, rank:]
    low_b_ref[: cols - half, :] = low_in_ref[half:cols, :] + update[half:, rank:]
    low_b_ref[cols - half :, :] = low_in_ref[cols:, :]
    out.wait()


def far_kernel(
    degree_hbm, dense_hbm, lu_hbm, ll_hbm,
    far_hbm,
    degree_ref, dense_ref, left_ref, spread_ref, far_ref, sems,
):
    leaves, block = degree_ref.shape
    rank = lu_hbm.shape[1]
    tiles = 4
    sides = [
        start(degree_hbm, degree_ref, sems.at[tiles]),
        start(lu_hbm, left_ref.at[:, pl.ds(0, rank)], sems.at[tiles + 1]),
        start(ll_hbm, left_ref.at[:, pl.ds(rank, rank)], sems.at[tiles + 2]),
    ]
    copies = load_tiles(dense_hbm, dense_ref, tiles, sems, 0)
    for side in sides:
        side.wait()
    columns = degree_columns(degree_ref)
    square = columns * columns
    for leaf in range(leaves):
        rows = slice(leaf * block, (leaf + 1) * block)
        spread_ref[rows, :] = scale_tile(square, leaf, left_ref[rows, :].astype(F32)).astype(BF16)
    for copy in copies:
        copy.wait()
    far_ref[...] = (DAMPING * dot(dense_ref[...], spread_ref[...])).astype(BF16)
    start(far_ref, far_hbm, sems.at[0]).wait()


def local_kernel(
    dense_hbm, known_hbm,
    local_hbm,
    dense_ref, known_ref, local_ref, sems,
):
    tiles = 4
    size = dense_ref.shape[0] // tiles
    copies = [
        pltpu.make_async_copy(
            dense_hbm.at[pl.ds(t * size, size)], dense_ref.at[pl.ds(t * size, size)], sems.at[t]
        )
        for t in range(tiles)
    ]
    known_copy = start(known_hbm, known_ref, sems.at[tiles])
    copies[0].start()
    copies[1].start()
    known_copy.wait()
    copies[2].start()
    copies[3].start()
    outs = []
    for half in range(2):
        copies[2 * half].wait()
        copies[2 * half + 1].wait()
        rows = slice(half * 2 * size, (half + 1) * 2 * size)
        near = pl.ds(half * 2 * size, 2 * size)
        local_ref[rows, :] = (DAMPING * dot(dense_ref[rows, :], known_ref[...])).astype(BF16)
        outs.append(start(local_ref.at[near], local_hbm.at[near], sems.at[half]))
    for out in outs:
        out.wait()


def final_kernel(
    inner, core_ref, degree_hbm, far_hbm, lu_hbm, ll_hbm, sib_hbm, y_hbm, local_hbm, mine_ref, other_ref, low_a_ref, low_b_ref,
    out_hbm,
    degree_ref, left_ref, coef_ref, sib_ref, own_ref, first_ref, second_ref, across_ref, low_ref, y_ref, local_ref, stage_ref, sems,
):
    tiles = 4
    rank = lu_hbm.shape[1]
    block = degree_ref.shape[1]
    size = stage_ref.shape[0] // tiles
    degree_copy = start(degree_hbm, degree_ref, sems.at[0])
    sib_copy = start(sib_hbm, sib_ref, sems.at[1])
    sides = [
        start(far_hbm, left_ref.at[:, pl.ds(0, 2 * rank)], sems.at[2]),
        start(lu_hbm, left_ref.at[:, pl.ds(2 * rank, rank)], sems.at[3]),
        start(ll_hbm, left_ref.at[:, pl.ds(3 * rank, rank)], sems.at[4]),
    ]
    loads = load_tiles(y_hbm, y_ref, tiles, sems, 5)
    others = load_tiles(local_hbm, local_ref, tiles, sems, 9)
    slots = mine_ref.shape[0]
    cols = own_ref.shape[0]
    width = cols // (2 * slots)
    lines = rank // (2 * slots)
    for source, core in ((mine_ref, core_ref[0]), (other_ref, 1 - core_ref[0])):
        for rest in range(slots // inner):
            some = source[rest * inner : (rest + 1) * inner]
            span = inner * width
            at = pl.ds(pl.multiple_of((2 * rest + core) * span, span), span)
            own_ref[at, :] = some[:, :width].reshape(span, rank)
            first_ref[at, :] = some[:, width : 2 * width].reshape(span, rank)
            second_ref[at, :] = some[:, 2 * width : 3 * width].reshape(span, rank)
            span = inner * lines
            at = pl.ds(pl.multiple_of((2 * rest + core) * span, span), span)
            across_ref[at, :] = some[:, 3 * width :].reshape(span, rank)
    half = low_a_ref.shape[0]
    low_ref[:half, :] = low_a_ref[...]
    low_ref[half:, :] = low_b_ref[...]
    first = first_ref[...]
    second = second_ref[...] + dot(
        own_ref[...].astype(BF16), (DAMPING * across_ref[...]).astype(BF16)
    )
    down = (DAMPING * low_ref[cols:, :]).astype(BF16)
    lower = low_ref[:cols, :] + dot(first.astype(BF16), down)
    sib_copy.wait()
    coef_ref[:, 0 * rank : 1 * rank] = (DAMPING * first).astype(BF16)
    coef_ref[:, 1 * rank : 2 * rank] = (DAMPING * sib_ref[...]).astype(BF16)
    coef_ref[:, 2 * rank : 3 * rank] = (DAMPING * second).astype(BF16)
    coef_ref[:, 3 * rank : 4 * rank] = (DAMPING * lower).astype(BF16)
    degree_copy.wait()
    columns = degree_columns(degree_ref)
    for side in sides:
        side.wait()
    outs = []
    for tile in range(tiles):
        rows = slice(tile * size, (tile + 1) * size)
        near = pl.ds(tile * size, size)
        product = lax.dot_general(
            left_ref[rows, :], coef_ref[...], (((1,), (1,)), ((), ())), preferred_element_type=F32
        )
        loads[tile].wait()
        others[tile].wait()
        stage_ref[rows, :] = y_ref[rows, :].astype(F32) + scale_tile(
            columns, tile * size // block, local_ref[rows, :].astype(F32) + product
        )
        outs.append(start(stage_ref.at[near], out_hbm.at[near], sems.at[tile]))
    for out in outs:
        out.wait()


def partner(value, axis, mask):
    pairs = [(source, source ^ mask) for source in range(lax.axis_size(axis))]
    return lax.ppermute(value, axis, pairs)


def low_bits(axis):
    masks = []
    while 2 ** (len(masks) + 1) < lax.axis_size(axis):
        masks.append(2 ** len(masks))
    return masks


def body(
    queries,
    inv_sqrt_degree,
    leaf_blocks,
    block_cols,
    left_upper,
    right_upper,
    left_lower,
    right_lower,
):
    inner = lax.axis_size("inner")
    parts = inner * lax.axis_size("rest") * lax.axis_size("core")
    rows, cols = queries.shape
    rank = left_upper.shape[1]
    leaves, stored, block, _ = leaf_blocks.shape
    degree = inv_sqrt_degree.reshape(leaves, block)
    width, lines = cols // parts, rank // parts
    height = 2 * width + lines
    node = ("rest", "core", "inner")
    dma = pltpu.SemaphoreType.DMA
    degree_scratch = pltpu.VMEM((leaves, block), F32)

    def scratch(*dims):
        return pltpu.VMEM(dims, BF16)

    def wide(*dims):
        return pltpu.VMEM(dims, F32)

    (first_lower,) = call(
        first_kernel,
        [(degree, FAR), (queries, FAR), (right_lower, FAR)],
        [shape((cols, rank), F32, True)],
        [degree_scratch, scratch(rows, cols), scratch(rows, rank), scratch(rows, cols), dma((6,))],
        8,
        2 * rows * cols * rank,
    )
    first_sib = [
        partner(first_lower, "inner", inner // 2 + other) for other in range(inner // 2)
    ]

    known, dense, both, low, lower_coupling = call(
        known_kernel,
        [(block_cols, FAR), (degree, FAR), (leaf_blocks, FAR), (queries, FAR)]
        + [(left_upper, FAR), (left_lower, FAR), (right_upper, FAR), (right_lower, FAR)],
        [
            shape((rows, cols), BF16),
            shape((rows, rows), BF16),
            shape((parts, height, rank), F32, True),
            shape((cols + rank, rank), F32, True),
            shape((rank, 2 * rank), F32, True),
        ],
        [pltpu.SMEM((leaves, stored), jnp.int32), degree_scratch]
        + [scratch(leaves, stored, block, block), scratch(rows, rows)]
        + [scratch(rows, cols)] * 3
        + [scratch(rows, 2 * rank)] * 3
        + [dma((11,))],
        36,
        2 * rows * rows * cols,
    )
    split = (cols + rank) // 2
    both, low_a, low_b, sib_lower = call(
        pack_kernel,
        [(both, VMEM), (low, VMEM), (lower_coupling, VMEM)] + [(value, VMEM) for value in first_sib],
        [
            shape((parts, height, rank), F32, True),
            shape((split, rank), F32, True),
            shape((cols + rank - split, rank), F32, True),
            shape((cols, rank), F32),
        ],
        [wide(cols, rank), dma(())],
        8,
        4 * cols * rank * rank,
    )
    both = lax.all_to_all(both, node, 0, 0, tiled=True)

    (far,) = call(
        far_kernel,
        [(degree, FAR), (dense, FAR), (left_upper, FAR), (left_lower, FAR)],
        [shape((rows, 2 * rank), BF16)],
        [degree_scratch, scratch(rows, rows)] + [scratch(rows, 2 * rank)] * 3 + [dma((7,))],
        20,
        4 * rows * rows * rank,
    )
    both, far = lax.optimization_barrier((both, far))
    both = both.sum(axis=0)
    received = partner(both, "node", 1)

    for mask in low_bits("inner"):
        low_a = low_a + partner(low_a, "inner", mask)
    low_b = partner(low_b, "inner", inner // 2)

    received, low_a, low_b, known = lax.optimization_barrier((received, low_a, low_b, known))
    sib = jnp.concatenate([both[:width], received], axis=0)
    sib = jnp.broadcast_to(sib[None], (parts // 2,) + sib.shape)
    sib = lax.all_to_all(sib, ("rest", "inner"), 0, 0, tiled=True)
    low_a = partner(low_a, "inner", inner // 2)
    for mask in low_bits("inner"):
        low_b = low_b + partner(low_b, "inner", mask)

    (local,) = call(
        local_kernel,
        [(dense, FAR), (known, FAR)],
        [shape((rows, cols), BF16)],
        [scratch(rows, rows), scratch(rows, cols), scratch(rows, cols), dma((5,))],
        20,
        2 * rows * rows * cols,
    )

    sib, local, low_a, low_b = lax.optimization_barrier((sib, local, low_a, low_b))
    other = partner(sib, "core", 1)
    core = lax.axis_index("core").astype(jnp.int32).reshape(1)
    (out,) = call(
        functools.partial(final_kernel, inner),
        [(core, SMEM), (degree, FAR), (far, FAR), (left_upper, FAR), (left_lower, FAR), (sib_lower, FAR)]
        + [(queries, FAR), (local, FAR), (sib, VMEM), (other, VMEM), (low_a, VMEM), (low_b, VMEM)],
        [shape((rows, cols), F32)],
        [degree_scratch, scratch(rows, 4 * rank), scratch(cols, 4 * rank)]
        + [wide(cols, rank)] * 4
        + [wide(rank, rank), wide(cols + rank, rank), scratch(rows, cols), scratch(rows, cols)]
        + [wide(rows, cols), dma((13,))],
        20,
        8 * rows * cols * rank,
    )
    return out


def solution(mesh):
    outer, inner = mesh.devices.shape
    fine = Mesh(mesh.devices.reshape(2, outer // 4, 2, inner), ("node", "rest", "core", "inner"))
    rows = P(("node", "rest", "core", "inner"))
    return jax.shard_map(
        body, mesh=fine, in_specs=(rows,) * 8, out_specs=rows, check_vma=False
    )
```

```python
import functools

import jax
import jax.numpy as jnp
from jax import lax
from jax.experimental import pallas as pl
from jax.experimental.pallas import tpu as pltpu
from jax.sharding import Mesh
from jax.sharding import PartitionSpec as P

DAMPING = 0.9
F32 = jnp.float32
BF16 = jnp.bfloat16
VMEM = pl.BlockSpec(memory_space=pltpu.VMEM)
SMEM = pl.BlockSpec(memory_space=pltpu.SMEM)
FAR = pl.BlockSpec(memory_space=pltpu.HBM)


def shape(dims, dtype, near=False):
    return (pltpu.VMEM if near else pltpu.HBM)(dims, dtype)


def call(kernel, args, outs, scratch, megabytes, flops):
    values = [
        value if spec is SMEM else pltpu.with_memory_space_constraint(value, spec.memory_space)
        for value, spec in args
    ]
    return pl.pallas_call(
        kernel,
        out_shape=[out for out in outs],
        in_specs=[spec for _, spec in args],
        out_specs=[
            FAR if out.memory_space == pltpu.HBM else VMEM for out in outs
        ],
        scratch_shapes=scratch,
        cost_estimate=pl.CostEstimate(
            flops=flops, bytes_accessed=2**20, transcendentals=0
        ),
        compiler_params=pltpu.CompilerParams(vmem_limit_bytes=megabytes * 2**20),
    )(*values)


def dot(a, b):
    return jnp.dot(a, b, preferred_element_type=F32)


def tdot(a, b):
    return lax.dot_general(a, b, (((0,), (0,)), ((), ())), preferred_element_type=F32)


def start(source, target, sem):
    copy = pltpu.make_async_copy(source, target, sem)
    copy.start()
    return copy


def degree_columns(degree_ref):
    leaves, block = degree_ref.shape
    tall = jnp.concatenate([degree_ref[...]] * (block // leaves), axis=0)
    return tall.T[:, :leaves]


def scale_tile(columns, first, value):
    block = columns.shape[0]
    return jnp.concatenate(
        [
            columns[:, first + b : first + b + 1] * value[b * block : (b + 1) * block]
            for b in range(value.shape[0] // block)
        ],
        axis=0,
    )


def load_tiles(hbm, ref, tiles, sems, first):
    size = ref.shape[0] // tiles
    return [
        start(hbm.at[pl.ds(t * size, size)], ref.at[pl.ds(t * size, size)], sems.at[first + t])
        for t in range(tiles)
    ]


def first_kernel(
    degree_hbm, y_hbm, rl_hbm,
    lower_ref,
    degree_ref, y_ref, right_ref, scaled_ref, sems,
):
    block = degree_ref.shape[1]
    tiles = 4
    size = y_ref.shape[0] // tiles
    degree_copy = start(degree_hbm, degree_ref, sems.at[tiles])
    right_copy = start(rl_hbm, right_ref, sems.at[tiles + 1])
    loads = load_tiles(y_hbm, y_ref, tiles, sems, 0)
    degree_copy.wait()
    columns = degree_columns(degree_ref)
    right_copy.wait()
    for tile in range(tiles):
        loads[tile].wait()
        rows = slice(tile * size, (tile + 1) * size)
        value = y_ref[rows, :].astype(F32)
        scaled_ref[rows, :] = scale_tile(columns, tile * size // block, value).astype(BF16)
    lower_ref[...] = tdot(scaled_ref[...], right_ref[...])


def place(cols_ref, blocks_ref, dense_ref):
    leaves, stored, block, _ = blocks_ref.shape
    for row in range(leaves):
        rows = slice(row * block, (row + 1) * block)
        dense_ref[rows, :] = jnp.zeros((block, leaves * block), BF16)
        for j in range(stored):
            col = pl.multiple_of(cols_ref[row, j] * block, block)
            dense_ref[rows, pl.ds(col, block)] = blocks_ref[row, j]


def known_kernel(
    cols_hbm, degree_hbm, blocks_hbm, y_hbm, lu_hbm, ll_hbm, ru_hbm, rl_hbm,
    known_hbm, dense_hbm, both_ref, low_ref, lower_coupling_ref,
    cols_ref, degree_ref, blocks_ref, dense_ref, y_ref, scaled_ref, known_ref, left_ref, spread_ref, right_ref, sems,
):
    leaves, _, block, _ = blocks_ref.shape
    rank = ru_hbm.shape[1]
    sides = [
        start(a, b, sems.at[i])
        for i, (a, b) in enumerate(
            (
                (degree_hbm, degree_ref),
                (cols_hbm, cols_ref),
                (lu_hbm, left_ref.at[:, pl.ds(0, rank)]),
                (ll_hbm, left_ref.at[:, pl.ds(rank, rank)]),
                (ru_hbm, right_ref.at[:, pl.ds(0, rank)]),
                (rl_hbm, right_ref.at[:, pl.ds(rank, rank)]),
                (y_hbm, y_ref),
            )
        )
    ]
    sides[0].wait()
    columns = degree_columns(degree_ref)
    square = columns * columns
    loads = load_tiles(blocks_hbm, blocks_ref, 4, sems, 7)
    for side in sides[1:]:
        side.wait()
    for leaf in range(leaves):
        rows = slice(leaf * block, (leaf + 1) * block)
        spread_ref[rows, :] = scale_tile(square, leaf, left_ref[rows, :].astype(F32)).astype(BF16)
        scaled_ref[rows, :] = scale_tile(columns, leaf, y_ref[rows, :].astype(F32)).astype(BF16)
    coupling = tdot(spread_ref[...], right_ref[...])
    parts, height, _ = both_ref.shape
    cols = scaled_ref.shape[1]
    width = cols // parts
    lines = rank // parts
    both_ref[:, :width, :] = tdot(scaled_ref[...], right_ref[:, :rank]).reshape(parts, width, rank)
    both_ref[:, 2 * width :, :] = coupling[:rank, :rank].reshape(parts, lines, rank)
    low_ref[cols:, :] = coupling[:rank, rank:]
    lower_coupling_ref[...] = coupling[rank:, :]
    for load in loads:
        load.wait()
    place(cols_ref, blocks_ref, dense_ref)
    outs = [start(dense_ref, dense_hbm, sems.at[0])]
    tiles = 4
    size = y_ref.shape[0] // tiles
    for tile in range(tiles):
        rows = slice(tile * size, (tile + 1) * size)
        first = tile * size // block
        product = dot(dense_ref[rows, :], scaled_ref[...])
        value = y_ref[rows, :].astype(F32) + DAMPING * scale_tile(columns, first, product)
        known_ref[rows, :] = scale_tile(columns, first, value).astype(BF16)
        if tile % 2 == 1:
            near = pl.ds((tile - 1) * size, 2 * size)
            outs.append(start(known_ref.at[near], known_hbm.at[near], sems.at[1 + tile]))
    found = tdot(known_ref[...], right_ref[...])
    low_ref[:cols, :] = found[:, rank:]
    both_ref[:, width : 2 * width, :] = found[:, :rank].reshape(parts, width, rank)
    for out in outs:
        out.wait()


def pack_kernel(*refs):
    both_in_ref, low_in_ref, coupling_ref = refs[:3]
    received = refs[3:-6]
    both_ref, low_a_ref, low_b_ref, sib_hbm, sib_ref, sem = refs[-6:]
    sib = received[0][...]
    for other in received[1:]:
        sib = sib + other[...]
    sib_ref[...] = sib
    out = start(sib_ref, sib_hbm, sem)
    cols, rank = sib.shape
    update = dot((DAMPING * sib).astype(BF16), coupling_ref[...].astype(BF16))
    parts, height, _ = both_ref.shape
    width = cols // parts
    both_ref[:, :width, :] = both_in_ref[:, :width, :]
    both_ref[:, 2 * width :, :] = both_in_ref[:, 2 * width :, :]
    both_ref[:, width : 2 * width, :] = both_in_ref[:, width : 2 * width, :] + update[
        :, :rank
    ].reshape(parts, width, rank)
    half = low_a_ref.shape[0]
    low_a_ref[...] = low_in_ref[:half, :] + update[:half, rank:]
    low_b_ref[: cols - half, :] = low_in_ref[half:cols, :] + update[half:, rank:]
    low_b_ref[cols - half :, :] = low_in_ref[cols:, :]
    out.wait()


def far_kernel(
    degree_hbm, dense_hbm, lu_hbm, ll_hbm,
    far_hbm,
    degree_ref, dense_ref, left_ref, spread_ref, far_ref, sems,
):
    leaves, block = degree_ref.shape
    rank = lu_hbm.shape[1]
    tiles = 4
    sides = [
        start(degree_hbm, degree_ref, sems.at[tiles]),
        start(lu_hbm, left_ref.at[:, pl.ds(0, rank)], sems.at[tiles + 1]),
        start(ll_hbm, left_ref.at[:, pl.ds(rank, rank)], sems.at[tiles + 2]),
    ]
    copies = load_tiles(dense_hbm, dense_ref, tiles, sems, 0)
    for side in sides:
        side.wait()
    columns = degree_columns(degree_ref)
    square = columns * columns
    for leaf in range(leaves):
        rows = slice(leaf * block, (leaf + 1) * block)
        spread_ref[rows, :] = scale_tile(square, leaf, left_ref[rows, :].astype(F32)).astype(BF16)
    for copy in copies:
        copy.wait()
    half = dense_ref.shape[0] // 2
    outs = []
    for part in range(2):
        rows = slice(part * half, (part + 1) * half)
        far_ref[rows, :] = (DAMPING * dot(dense_ref[rows, :], spread_ref[...])).astype(BF16)
        near = pl.ds(part * half, half)
        outs.append(start(far_ref.at[near], far_hbm.at[near], sems.at[part]))
    for out in outs:
        out.wait()


def local_kernel(
    dense_hbm, known_hbm,
    local_hbm,
    dense_ref, known_ref, local_ref, sems,
):
    tiles = 4
    size = dense_ref.shape[0] // tiles
    copies = [
        pltpu.make_async_copy(
            dense_hbm.at[pl.ds(t * size, size)], dense_ref.at[pl.ds(t * size, size)], sems.at[t]
        )
        for t in range(tiles)
    ]
    known_copy = start(known_hbm, known_ref, sems.at[tiles])
    copies[0].start()
    copies[1].start()
    known_copy.wait()
    copies[2].start()
    copies[3].start()
    outs = []
    for half in range(2):
        copies[2 * half].wait()
        copies[2 * half + 1].wait()
        rows = slice(half * 2 * size, (half + 1) * 2 * size)
        near = pl.ds(half * 2 * size, 2 * size)
        for tile in (2 * half, 2 * half + 1):
            rows = slice(tile * size, (tile + 1) * size)
            near = pl.ds(tile * size, size)
            local_ref[rows, :] = (DAMPING * dot(dense_ref[rows, :], known_ref[...])).astype(BF16)
            outs.append(start(local_ref.at[near], local_hbm.at[near], sems.at[tile]))
    for out in outs:
        out.wait()


def final_kernel(
    inner, core_ref, degree_hbm, far_hbm, lu_hbm, ll_hbm, sib_hbm, y_hbm, local_hbm, mine_ref, other_ref, low_a_ref, low_b_ref,
    out_hbm,
    degree_ref, left_ref, coef_ref, sib_ref, own_ref, first_ref, second_ref, across_ref, low_ref, y_ref, local_ref, stage_ref, sems,
):
    tiles = 4
    rank = lu_hbm.shape[1]
    block = degree_ref.shape[1]
    size = stage_ref.shape[0] // tiles
    degree_copy = start(degree_hbm, degree_ref, sems.at[0])
    sib_copy = start(sib_hbm, sib_ref, sems.at[1])
    sides = [
        start(far_hbm, left_ref.at[:, pl.ds(0, 2 * rank)], sems.at[2]),
        start(lu_hbm, left_ref.at[:, pl.ds(2 * rank, rank)], sems.at[3]),
        start(ll_hbm, left_ref.at[:, pl.ds(3 * rank, rank)], sems.at[4]),
    ]
    loads = load_tiles(y_hbm, y_ref, tiles, sems, 5)
    others = load_tiles(local_hbm, local_ref, tiles, sems, 9)
    slots = mine_ref.shape[0]
    cols = own_ref.shape[0]
    width = cols // (2 * slots)
    lines = rank // (2 * slots)
    for source, core in ((mine_ref, core_ref[0]), (other_ref, 1 - core_ref[0])):
        for rest in range(slots // inner):
            some = source[rest * inner : (rest + 1) * inner]
            span = inner * width
            at = pl.ds(pl.multiple_of((2 * rest + core) * span, span), span)
            own_ref[at, :] = some[:, :width].reshape(span, rank)
            first_ref[at, :] = some[:, width : 2 * width].reshape(span, rank)
            second_ref[at, :] = some[:, 2 * width : 3 * width].reshape(span, rank)
            span = inner * lines
            at = pl.ds(pl.multiple_of((2 * rest + core) * span, span), span)
            across_ref[at, :] = some[:, 3 * width :].reshape(span, rank)
    half = low_a_ref.shape[0]
    low_ref[:half, :] = low_a_ref[...]
    low_ref[half:, :] = low_b_ref[...]
    first = first_ref[...]
    second = second_ref[...] + dot(
        own_ref[...].astype(BF16), (DAMPING * across_ref[...]).astype(BF16)
    )
    down = (DAMPING * low_ref[cols:, :]).astype(BF16)
    lower = low_ref[:cols, :] + dot(first.astype(BF16), down)
    sib_copy.wait()
    coef_ref[:, 0 * rank : 1 * rank] = (DAMPING * first).astype(BF16)
    coef_ref[:, 1 * rank : 2 * rank] = (DAMPING * sib_ref[...]).astype(BF16)
    coef_ref[:, 2 * rank : 3 * rank] = (DAMPING * second).astype(BF16)
    coef_ref[:, 3 * rank : 4 * rank] = (DAMPING * lower).astype(BF16)
    degree_copy.wait()
    columns = degree_columns(degree_ref)
    for side in sides:
        side.wait()
    outs = []
    for tile in range(tiles):
        rows = slice(tile * size, (tile + 1) * size)
        near = pl.ds(tile * size, size)
        product = lax.dot_general(
            left_ref[rows, :], coef_ref[...], (((1,), (1,)), ((), ())), preferred_element_type=F32
        )
        loads[tile].wait()
        others[tile].wait()
        stage_ref[rows, :] = y_ref[rows, :].astype(F32) + scale_tile(
            columns, tile * size // block, local_ref[rows, :].astype(F32) + product
        )
        outs.append(start(stage_ref.at[near], out_hbm.at[near], sems.at[tile]))
    for out in outs:
        out.wait()


def partner(value, axis, mask):
    pairs = [(source, source ^ mask) for source in range(lax.axis_size(axis))]
    return lax.ppermute(value, axis, pairs)


def low_bits(axis):
    masks = []
    while 2 ** (len(masks) + 1) < lax.axis_size(axis):
        masks.append(2 ** len(masks))
    return masks


def body(
    queries,
    inv_sqrt_degree,
    leaf_blocks,
    block_cols,
    left_upper,
    right_upper,
    left_lower,
    right_lower,
):
    inner = lax.axis_size("inner")
    parts = inner * lax.axis_size("rest") * lax.axis_size("core")
    rows, cols = queries.shape
    rank = left_upper.shape[1]
    leaves, stored, block, _ = leaf_blocks.shape
    degree = inv_sqrt_degree.reshape(leaves, block)
    width, lines = cols // parts, rank // parts
    height = 2 * width + lines
    node = ("rest", "core", "inner")
    dma = pltpu.SemaphoreType.DMA
    degree_scratch = pltpu.VMEM((leaves, block), F32)

    def scratch(*dims):
        return pltpu.VMEM(dims, BF16)

    def wide(*dims):
        return pltpu.VMEM(dims, F32)

    (first_lower,) = call(
        first_kernel,
        [(degree, FAR), (queries, FAR), (right_lower, FAR)],
        [shape((cols, rank), F32, True)],
        [degree_scratch, scratch(rows, cols), scratch(rows, rank), scratch(rows, cols), dma((6,))],
        8,
        2 * rows * cols * rank,
    )
    first_sib = [
        partner(first_lower, "inner", inner // 2 + other) for other in range(inner // 2)
    ]

    known, dense, both, low, lower_coupling = call(
        known_kernel,
        [(block_cols, FAR), (degree, FAR), (leaf_blocks, FAR), (queries, FAR)]
        + [(left_upper, FAR), (left_lower, FAR), (right_upper, FAR), (right_lower, FAR)],
        [
            shape((rows, cols), BF16),
            shape((rows, rows), BF16),
            shape((parts, height, rank), F32, True),
            shape((cols + rank, rank), F32, True),
            shape((rank, 2 * rank), F32, True),
        ],
        [pltpu.SMEM((leaves, stored), jnp.int32), degree_scratch]
        + [scratch(leaves, stored, block, block), scratch(rows, rows)]
        + [scratch(rows, cols)] * 3
        + [scratch(rows, 2 * rank)] * 3
        + [dma((11,))],
        36,
        2 * rows * rows * cols,
    )
    split = (cols + rank) // 2
    both, low_a, low_b, sib_lower = call(
        pack_kernel,
        [(both, VMEM), (low, VMEM), (lower_coupling, VMEM)] + [(value, VMEM) for value in first_sib],
        [
            shape((parts, height, rank), F32, True),
            shape((split, rank), F32, True),
            shape((cols + rank - split, rank), F32, True),
            shape((cols, rank), F32),
        ],
        [wide(cols, rank), dma(())],
        8,
        4 * cols * rank * rank,
    )
    both = lax.all_to_all(both, node, 0, 0, tiled=True)

    (far,) = call(
        far_kernel,
        [(degree, FAR), (dense, FAR), (left_upper, FAR), (left_lower, FAR)],
        [shape((rows, 2 * rank), BF16)],
        [degree_scratch, scratch(rows, rows)] + [scratch(rows, 2 * rank)] * 3 + [dma((7,))],
        20,
        4 * rows * rows * rank,
    )
    both, far = lax.optimization_barrier((both, far))
    both = both.sum(axis=0)
    received = partner(both, "node", 1)

    for mask in low_bits("inner"):
        low_a = low_a + partner(low_a, "inner", mask)
    low_b = partner(low_b, "inner", inner // 2)

    received, low_a, low_b, known = lax.optimization_barrier((received, low_a, low_b, known))
    sib = jnp.concatenate([both[:width], received], axis=0)
    sib = jnp.broadcast_to(sib[None], (parts // 2,) + sib.shape)
    sib = lax.all_to_all(sib, ("rest", "inner"), 0, 0, tiled=True)
    low_a = partner(low_a, "inner", inner // 2)
    for mask in low_bits("inner"):
        low_b = low_b + partner(low_b, "inner", mask)

    (local,) = call(
        local_kernel,
        [(dense, FAR), (known, FAR)],
        [shape((rows, cols), BF16)],
        [scratch(rows, rows), scratch(rows, cols), scratch(rows, cols), dma((5,))],
        20,
        2 * rows * rows * cols,
    )

    sib, local, low_a, low_b = lax.optimization_barrier((sib, local, low_a, low_b))
    other = partner(sib, "core", 1)
    core = lax.axis_index("core").astype(jnp.int32).reshape(1)
    (out,) = call(
        functools.partial(final_kernel, inner),
        [(core, SMEM), (degree, FAR), (far, FAR), (left_upper, FAR), (left_lower, FAR), (sib_lower, FAR)]
        + [(queries, FAR), (local, FAR), (sib, VMEM), (other, VMEM), (low_a, VMEM), (low_b, VMEM)],
        [shape((rows, cols), F32)],
        [degree_scratch, scratch(rows, 4 * rank), scratch(cols, 4 * rank)]
        + [wide(cols, rank)] * 4
        + [wide(rank, rank), wide(cols + rank, rank), scratch(rows, cols), scratch(rows, cols)]
        + [wide(rows, cols), dma((13,))],
        20,
        8 * rows * cols * rank,
    )
    return out


def solution(mesh):
    outer, inner = mesh.devices.shape
    fine = Mesh(mesh.devices.reshape(2, outer // 4, 2, inner), ("node", "rest", "core", "inner"))
    rows = P(("node", "rest", "core", "inner"))
    return jax.shard_map(
        body, mesh=fine, in_specs=(rows,) * 8, out_specs=rows, check_vma=False
    )
```
